32 devices in a mesh: row: 16 (over z, y, x), col: 2 (over core).
Axes of the slice: x: 2, y: 2, z: 4, core: 2. Of those that a mesh axis runs over, the one named last changes fastest.
Arguments:
- kernel: float32 [1024, 65536], P('row', 'col'), may hold values from -6 to 6
- basis: float32 [65536, 128], P('col', 'row'), may hold values from -0.0234375 to 0.0234375
- responses: float32 [1024, 512], P('row', 'col'), may hold values from -6 to 6
Outputs:
- scores: float32 [1024, 128], P('row')
- loadings: float32 [128, 65536], P('row', 'col')
- weights: float32 [512, 128], P('col')
- deflated: float32 [1024, 65536], P('row', 'col')
- basis_next: float32 [1024, 128], P('row')
The draws below stay inside these ranges and needn't reach their ends.
All inputs are finite; a program needn't handle non-finite values.
Results may differ from the reference program's by a relative error of at most 0.00012.
Values sent between devices are 32-bit elements; how exact they have to be, the bound alone decides.
A program may use at most 64 MiB of HBM per device.

```python
import math
import jax
import jax.numpy as jnp
from jax import lax

N = 65536
COMP = 128
M = 512
ROWS = 1024


def steps_of(own_key, dims, pieces, least, high):
    gain = 1.0
    for dim, blocks in pieces:
        steps = jax.random.uniform(jax.random.fold_in(jax.random.fold_in(own_key, 6), dim), (blocks,), jnp.float32, least / len(pieces), high / len(pieces))
        gain = gain * jnp.repeat(jnp.exp(steps), dims[dim] // blocks).reshape((-1,) + (1,) * (len(dims) - 1 - dim))
    return gain


def centred(key, dims, spread, limit, split=(), held_as=jnp.bfloat16):
    loudness = steps_of(key, dims, split, -0.22, 0.18) if split else 1.0
    result = jax.random.normal(key, dims, jnp.float32) * spread * loudness
    return jnp.minimum(jnp.maximum(result, -limit), limit).astype(held_as)


def setup_inputs(seed: int = 0) -> dict:
    key_of = jax.random.split(jax.random.key(seed), 4)
    kernel = centred(key_of[0], (ROWS, N), 1.0, 6.0, ((0, 16), (1, 2)), jnp.float32)
    basis = centred(key_of[1], (N, COMP), N ** -0.5, 0.0234375, ((0, 2), (1, 16)), jnp.float32)
    responses = centred(key_of[2], (ROWS, M), 1.0, 6.0, ((0, 16), (1, 2)), jnp.float32)
    return dict(kernel=kernel, basis=basis, responses=responses)


def reference(kernel, basis, responses):
    highest = lax.Precision.HIGHEST
    root_rows = math.sqrt(ROWS)
    projected = jnp.dot(kernel, basis, precision=highest)
    gram_mat = jnp.dot(projected.T, projected, precision=highest) / ROWS
    factor = jnp.linalg.cholesky(gram_mat)
    scores = jax.scipy.linalg.solve_triangular(factor, projected.T, lower=True).T
    loadings = jnp.dot(scores.T, kernel, precision=highest) / root_rows
    deflated = kernel - jnp.dot(scores, loadings, precision=highest) / root_rows
    weights = jnp.dot(responses.T, scores, precision=highest) / root_rows
    basis_next = jnp.dot(responses, weights, precision=highest) / math.sqrt(M)
    return (scores, loadings, weights, deflated, basis_next)
```

```python
import math

import jax
import jax.numpy as jnp
from jax import lax
from jax.experimental import pallas as pl
from jax.experimental.pallas import tpu as pltpu
from jax.sharding import PartitionSpec as P

MESH = pl.DeviceIdType.MESH
HIGHEST = lax.Precision.HIGHEST
PLANE = 4
LAST = (((1,), (1,)), ((), ()))
FIRST = (((0,), (0,)), ((), ()))
PLAIN = (((1,), (0,)), ((), ()))


def dot(a, b, dims):
    return lax.dot_general(a, b, dims, precision=HIGHEST, preferred_element_type=jnp.float32)


def chunks_of(width, most):
    return max(c for c in range(1, most + 1) if width % (c * 128) == 0)


def remote(src, dst, send, recv, device):
    return pltpu.make_async_remote_copy(
        src_ref=src,
        dst_ref=dst,
        send_sem=send,
        recv_sem=recv,
        device_id=device,
        device_id_type=MESH,
    )


def done(ref, sem):
    pltpu.make_async_copy(ref, ref, sem).wait()


def inverse_factor(work, inverse, comp):
    lane = lax.broadcasted_iota(jnp.int32, (8, comp), 1)
    sub = lax.broadcasted_iota(jnp.int32, (8, 1), 0)

    def panel(p, carry):
        top = pl.multiple_of(p * 8, 8)
        left = work[pl.ds(top, 8), :comp]
        right = work[pl.ds(top, 8), comp:]
        cols = [
            jnp.sum(jnp.where(lane == top + j, left, 0.0), axis=1, keepdims=True) for j in range(8)
        ]
        for j in range(8):
            scale = 1.0 / jnp.sqrt(cols[j][j : j + 1, :])
            mult = jnp.where(sub > j, cols[j] * scale, 0.0)
            left_row = left[j : j + 1, :] * scale
            right_row = right[j : j + 1, :] * scale
            left = jnp.where(sub == j, left_row, left - mult * left_row)
            right = jnp.where(sub == j, right_row, right - mult * right_row)
            for m in range(j + 1, 8):
                cols[m] = cols[m] - mult * (cols[m][j : j + 1, :] * scale)
        inverse[pl.ds(top, 8), :] = right
        work[...] = work[...] - dot(left, jnp.concatenate([left, right], axis=1), FIRST)
        return carry

    lax.fori_loop(0, comp // 8, panel, 0)


def step(kernel, basis_t, responses):
    n, cols = lax.axis_size("row"), lax.axis_size("col")
    planes = n // PLANE
    height, total = kernel.shape
    here = basis_t.shape[0]
    comp = here * n
    resp = responses.shape[1]
    width = total // PLANE
    rows = height * PLANE
    group = PLANE * cols
    slab = rows // group
    gram_slab = comp // PLANE
    resp_slab = resp // PLANE
    root_rows = math.sqrt(height * n)
    root_resp = math.sqrt(resp * cols)
    nk = chunks_of(width, 8)
    wk = width // nk
    nm = chunks_of(width, 16)
    wm = width // nm
    ahead_k, ahead_b, ahead_m = min(2, nk), min(2, nk), min(3, nm)
    half = planes // 2

    def body(
        k_hbm,
        b_hbm,
        resp_ref,
        scores,
        loadings,
        weights,
        deflated,
        nxt,
        kx,
        bq,
        acc,
        outer,
        tot,
        lbuf,
        part,
        part_in,
        full,
        full_t,
        gram,
        gram_in,
        gram_sum,
        gram_full,
        work,
        inverse,
        mix,
        t_own,
        t_in,
        t_sum,
        t_z,
        t_full,
        next_own,
        next_in,
        k_send,
        k_recv,
        b_send,
        b_recv,
        zb_send,
        zb_recv,
        p_send,
        p_recv,
        f_send,
        f_recv,
        g_send,
        g_recv,
        gf_send,
        gf_recv,
        t_send,
        t_recv,
        tz_send,
        tz_recv,
        tf_send,
        tf_recv,
        n_send,
        n_recv,
        in_send,
        in_recv,
        tot_send,
        tot_recv,
        d_send,
        d_recv,
        l_send,
        l_recv,
    ):
        me, col = lax.axis_index("row"), lax.axis_index("col")
        z, q = me // PLANE, me % PLANE
        y, x = q // 2, q % 2

        def peer(k):
            return (1 - y if k & 2 else y) * 2 + (1 - x if k & 1 else x)

        peers = [peer(k) for k in range(PLANE)]
        mine = q * cols + col

        def member(d):
            other = lax.rem(mine + d, group)
            return other, {"row": z * PLANE + other // cols, "col": other % cols}

        def plane_of(d):
            return lax.rem(z + d, planes)

        def above(f):
            pl.when(z < planes - 1)(f)

        def below(f):
            pl.when(z > 0)(f)

        def span(c, w):
            return pl.ds(pl.multiple_of(c * w, w), w)

        def quarter(k, c, w):
            return pl.ds(pl.multiple_of(peers[k] * width + c * w, w), w)

        def k_copy(c, k):
            src = k_hbm.at[:, quarter(k, c, wk)]
            dst = kx.at[q, :, span(c, wk)]
            if k == 0:
                return pltpu.make_async_copy(src, dst, k_recv.at[c, 0])
            return remote(
                src, dst, k_send.at[k], k_recv.at[c, k], {"row": z * PLANE + peers[k]}
            )

        def b_copy(c, k):
            src = b_hbm.at[:, quarter(k, c, wk)]
            dst = bq.at[me, :, span(c, wk)]
            if k == 0:
                return pltpu.make_async_copy(src, dst, b_recv.at[c, 0])
            return remote(
                src, dst, b_send.at[k], b_recv.at[c, k], {"row": z * PLANE + peers[k]}
            )

        def bz_block(c, origin):
            return bq.at[pl.ds(origin * PLANE, PLANE), :, span(c, wk)]

        def bz_copy(c, origin, way):
            ref = bz_block(c, origin)
            return remote(
                ref,
                ref,
                zb_send.at[(way + 1) // 2, c, origin],
                zb_recv.at[c, origin],
                {"row": me + way * PLANE},
            )

        def bz_first(c):
            for k in range(PLANE):
                done(bq.at[z * PLANE + peers[k], :, span(c, wk)], b_recv.at[c, k])

            @above
            def _():
                bz_copy(c, z, 1).start()

            @below
            def _():
                bz_copy(c, z, -1).start()

        def bz_relay(c):
            for d in range(1, planes):

                @pl.when(z - d >= 0)
                def _(d=d):
                    done(bz_block(c, z - d), zb_recv.at[c, z - d])

                    @above
                    def _():
                        bz_copy(c, z - d, 1).start()

                @pl.when(z + d < planes)
                def _(d=d):
                    done(bz_block(c, z + d), zb_recv.at[c, z + d])

                    @below
                    def _():
                        bz_copy(c, z + d, -1).start()

        b_own = [b_copy(c, 0) for c in range(nk)]
        for copy in b_own:
            copy.start()

        def k_own(c, carry):
            k_copy(c, 0).start()
            return carry

        lax.fori_loop(0, nk, k_own, 0)

        barrier = pltpu.get_barrier_semaphore()
        for d in range(1, group):
            pl.semaphore_signal(barrier, inc=1, device_id=member(d)[1], device_id_type=MESH)
        for d in range(1, planes):
            pl.semaphore_signal(
                barrier,
                inc=1,
                device_id={"row": plane_of(d) * PLANE + q},
                device_id_type=MESH,
            )
        pl.semaphore_wait(barrier, group + planes - 2)

        def b_start(c, carry):
            for k in range(1, PLANE):
                b_copy(c, k).start()
            return carry

        lax.fori_loop(0, nk, b_start, 0)
        for c in range(ahead_k):
            for k in range(1, PLANE):
                k_copy(c, k).start()
        for c in range(ahead_b):
            bz_first(c)
        part[...] = jnp.zeros_like(part)

        def project(c, carry):
            @pl.when(c + ahead_k < nk)
            def _():
                for k in range(1, PLANE):
                    k_copy(c + ahead_k, k).start()

            @pl.when(c + ahead_b < nk)
            def _():
                bz_first(c + ahead_b)

            bz_relay(c)
            for k in range(PLANE):
                done(kx.at[peers[k], :, span(c, wk)], k_recv.at[c, k])
            here_k = kx[:, :, span(c, wk)].reshape(rows, wk)
            here_b = bq[:, :, span(c, wk)].reshape(comp, wk)
            part[...] += dot(here_k, here_b, LAST).reshape(part.shape)
            return carry

        lax.fori_loop(0, nk, project, 0)

        for d in range(1, group):
            other, device = member(d)
            remote(
                part.at[other], part_in.at[mine], p_send.at[other], p_recv.at[mine], device
            ).start()
        total_rows = part[mine]
        for d in range(1, group):
            other, _ = member(d)
            done(part_in.at[other], p_recv.at[other])
            total_rows = total_rows + part_in[other]
        full[mine] = total_rows
        for d in range(1, group):
            other, device = member(d)
            remote(
                full.at[mine], full.at[mine], f_send.at[other], f_recv.at[mine], device
            ).start()
        for d in range(1, group):
            other, _ = member(d)
            done(full.at[other], f_recv.at[other])
        projected = full[...].reshape(rows, comp)

        gram[...] = dot(projected, projected, FIRST).reshape(gram.shape)

        def g_copy(d):
            return remote(
                gram.at[q],
                gram_in.at[z],
                g_send.at[plane_of(d)],
                g_recv.at[z],
                {"row": plane_of(d) * PLANE + q},
            )

        for d in range(1, planes):
            g_copy(d).start()
        gram_in[z] = gram[q]
        full_t[...] = projected.T

        lower = z < half
        inner_z = jnp.where(lower, z + 1, z - 1)
        outer_z = jnp.where(lower, z - 1, z + 1)
        centre = jnp.logical_or(z == half - 1, z == half)
        inward = {"row": inner_z * PLANE + q}
        outward = {"row": outer_z * PLANE + q}
        has_outer = jnp.logical_and(z > 0, z < planes - 1)

        def in_copy(c, to, recv):
            return remote(
                acc.at[:, span(c, wm)], to.at[:, span(c, wm)], in_send.at[c], recv.at[c], inward
            )

        def tot_copy(c):
            ref = tot.at[:, span(c, wm)]
            return remote(ref, ref, tot_send.at[c], tot_recv.at[c], outward)

        def gather_in(c):
            own = dot(full_t[...], kx[:, :, span(c, wm)].reshape(rows, wm), PLAIN)
            acc[:, span(c, wm)] = own

            @pl.when(has_outer)
            def _():
                done(outer.at[:, span(c, wm)], in_recv.at[c])
                acc[:, span(c, wm)] = acc[:, span(c, wm)] + outer[:, span(c, wm)]

            @pl.when(centre)
            def _():
                in_copy(c, tot, tot_recv).start()

            @pl.when(jnp.logical_not(centre))
            def _():
                in_copy(c, outer, in_recv).start()

        for c in range(min(1, nm)):
            gather_in(c)

        for d in range(1, planes):
            done(gram_in.at[plane_of(d)], g_recv.at[plane_of(d)])
        gram_full[q] = jnp.sum(gram_in[...], axis=0)

        def gf_copy(k):
            return remote(
                gram_full.at[q],
                gram_full.at[q],
                gf_send.at[k],
                gf_recv.at[k],
                {"row": z * PLANE + peers[k]},
            )

        for k in range(1, PLANE):
            gf_copy(k).start()

        own_rows = full[pl.ds(q * cols, cols)].reshape(height, comp)
        t_own[...] = dot(resp_ref[...], own_rows, FIRST).reshape(t_own.shape)
        for k in range(1, PLANE):
            remote(
                t_own.at[peers[k]],
                t_in.at[q],
                t_send.at[k],
                t_recv.at[k],
                {"row": z * PLANE + peers[k]},
            ).start()
        t_in[q] = t_own[q]
        for k in range(1, PLANE):
            done(gram_full.at[peers[k]], gf_recv.at[k])
        work[:, :comp] = gram_full[...].reshape(comp, comp) * (1.0 / (height * n))
        work[:, comp:] = (
            lax.broadcasted_iota(jnp.int32, (comp, comp), 0)
            == lax.broadcasted_iota(jnp.int32, (comp, comp), 1)
        ).astype(jnp.float32)
        inverse_factor(work, inverse, comp)
        plane_scores = dot(projected, inverse[...], LAST)
        mix[pl.ds(0, rows), :] = dot(plane_scores, inverse[...], PLAIN) * (1.0 / (height * n))
        mix[pl.ds(rows, here * PLANE), :] = inverse[
            pl.ds(pl.multiple_of(z * (here * PLANE), here * PLANE), here * PLANE), :
        ] * (1.0 / root_rows)
        scores[...] = dot(own_rows, inverse[...], LAST)

        for k in range(1, PLANE):
            done(t_in.at[peers[k]], t_recv.at[k])
        t_z[z] = jnp.sum(t_in[...], axis=0)
        t_sum[...] = t_z[z]
        for d in range(1, planes):
            remote(
                t_sum,
                t_z.at[z],
                tz_send.at[plane_of(d)],
                tz_recv.at[z],
                {"row": plane_of(d) * PLANE + q},
            ).start()

        for c in range(1, ahead_m):
            gather_in(c)

        def d_copy(c, k):
            src = kx.at[peers[k], :, span(c, wm)]
            dst = deflated.at[:, quarter(0, c, wm)]
            if k == 0:
                return pltpu.make_async_copy(src, dst, d_recv.at[0])
            return remote(src, dst, d_send.at[k], d_recv.at[k], {"row": z * PLANE + peers[k]})

        def l_copy(c, k):
            src = lbuf.at[peers[k], :, span(c, wm)]
            dst = loadings.at[:, quarter(0, c, wm)]
            if k == 0:
                return pltpu.make_async_copy(src, dst, l_recv.at[0])
            return remote(src, dst, l_send.at[k], l_recv.at[k], {"row": z * PLANE + peers[k]})

        def deflate(c, carry):
            @pl.when(c + ahead_m < nm)
            def _():
                gather_in(c + ahead_m)

            done(tot.at[:, span(c, wm)], tot_recv.at[c])

            @pl.when(centre)
            def _():
                tot[:, span(c, wm)] = tot[:, span(c, wm)] + acc[:, span(c, wm)]

            @pl.when(has_outer)
            def _():
                tot_copy(c).start()

            product = dot(mix[...], tot[:, span(c, wm)], PLAIN)
            kx[:, :, span(c, wm)] = kx[:, :, span(c, wm)] - product[:rows].reshape(
                PLANE, height, wm
            )
            lbuf[:, :, span(c, wm)] = product[rows:].reshape(PLANE, here, wm)
            for k in (3, 1, 2, 0):
                d_copy(c, k).start()
                l_copy(c, k).start()
            return carry

        lax.fori_loop(0, nm, deflate, 0)

        for d in range(1, planes):
            done(t_z.at[plane_of(d)], tz_recv.at[plane_of(d)])
        t_full[q] = jnp.sum(t_z[...], axis=0)
        for k in range(1, PLANE):
            remote(
                t_full.at[q],
                t_full.at[q],
                tf_send.at[k],
                tf_recv.at[k],
                {"row": z * PLANE + peers[k]},
            ).start()
        for k in range(1, PLANE):
            done(t_full.at[peers[k]], tf_recv.at[k])
        weights_here = dot(t_full[...].reshape(resp, comp), inverse[...], LAST) * (1.0 / root_rows)
        weights[...] = weights_here
        next_own[...] = dot(resp_ref[...], weights_here, PLAIN) * (1.0 / root_resp)
        next_in[col] = next_own[...]
        for d in range(1, cols):
            there = lax.rem(col + d, cols)
            remote(
                next_own, next_in.at[col], n_send.at[there], n_recv.at[col], {"col": there}
            ).start()
        for d in range(1, cols):
            there = lax.rem(col + d, cols)
            done(next_in.at[there], n_recv.at[there])
        nxt[...] = jnp.sum(next_in[...], axis=0)

        for k in range(PLANE):
            done(deflated.at[:, pl.ds(pl.multiple_of(peers[k] * width, width), width)], d_recv.at[k])
            done(loadings.at[:, pl.ds(pl.multiple_of(peers[k] * width, width), width)], l_recv.at[k])
        for k in range(1, PLANE):
            done(kx.at[0], k_send.at[k])
            done(bq.at[0], b_send.at[k])
            done(kx.at[0], d_send.at[k])
            done(lbuf.at[0], l_send.at[k])
            done(t_own.at[0], t_send.at[k])
            done(t_full.at[0], tf_send.at[k])
            done(gram_full.at[0], gf_send.at[k])
        for d in range(1, group):
            other, _ = member(d)
            done(part.at[0], p_send.at[other])
            done(full.at[0], f_send.at[other])
        for d in range(1, planes):
            done(gram.at[0], g_send.at[plane_of(d)])
            done(t_sum, tz_send.at[plane_of(d)])
        for d in range(1, cols):
            done(next_own, n_send.at[lax.rem(col + d, cols)])

        def b_end(c, carry):
            for o in range(planes):

                @pl.when(jnp.logical_and(z < planes - 1, o <= z))
                def _(o=o):
                    done(bz_block(c, o), zb_send.at[1, c, o])

                @pl.when(jnp.logical_and(z > 0, o >= z))
                def _(o=o):
                    done(bz_block(c, o), zb_send.at[0, c, o])

            return carry

        lax.fori_loop(0, nk, b_end, 0)

        def m_end(c, carry):
            done(acc.at[:, span(c, wm)], in_send.at[c])

            @pl.when(has_outer)
            def _():
                done(tot.at[:, span(c, wm)], tot_send.at[c])

            return carry

        lax.fori_loop(0, nm, m_end, 0)

    f32 = jnp.float32
    dma = pltpu.SemaphoreType.DMA
    vmem = pl.BlockSpec(memory_space=pltpu.VMEM)
    anywhere = pl.BlockSpec(memory_space=pl.ANY)
    return pl.pallas_call(
        body,
        out_shape=[
            jax.ShapeDtypeStruct((height, comp), f32),
            jax.ShapeDtypeStruct((here, total), f32),
            jax.ShapeDtypeStruct((resp, comp), f32),
            jax.ShapeDtypeStruct((height, total), f32),
            jax.ShapeDtypeStruct((height, comp), f32),
        ],
        in_specs=[anywhere, anywhere, vmem],
        out_specs=[vmem, anywhere, vmem, anywhere, vmem],
        scratch_shapes=[
            pltpu.VMEM((PLANE, height, width), f32),
            pltpu.VMEM((n, here, width), f32),
            pltpu.VMEM((comp, width), f32),
            pltpu.VMEM((comp, width), f32),
            pltpu.VMEM((comp, width), f32),
            pltpu.VMEM((PLANE, here, width), f32),
            pltpu.VMEM((group, slab, comp), f32),
            pltpu.VMEM((group, slab, comp), f32),
            pltpu.VMEM((group, slab, comp), f32),
            pltpu.VMEM((comp, rows), f32),
            pltpu.VMEM((PLANE, gram_slab, comp), f32),
            pltpu.VMEM((planes, gram_slab, comp), f32),
            pltpu.VMEM((gram_slab, comp), f32),
            pltpu.VMEM((PLANE, gram_slab, comp), f32),
            pltpu.VMEM((comp, 2 * comp), f32),
            pltpu.VMEM((comp, comp), f32),
            pltpu.VMEM((rows + here * PLANE, comp), f32),
            pltpu.VMEM((PLANE, resp_slab, comp), f32),
            pltpu.VMEM((PLANE, resp_slab, comp), f32),
            pltpu.VMEM((resp_slab, comp), f32),
            pltpu.VMEM((planes, resp_slab, comp), f32),
            pltpu.VMEM((PLANE, resp_slab, comp), f32),
            pltpu.VMEM((height, comp), f32),
            pltpu.VMEM((cols, height, comp), f32),
            dma((PLANE,)),
            dma((nk, PLANE)),
            dma((PLANE,)),
            dma((nk, PLANE)),
            dma((2, nk, planes)),
            dma((nk, planes)),
            dma((group,)),
            dma((group,)),
            dma((group,)),
            dma((group,)),
            dma((planes,)),
            dma((planes,)),
            dma((PLANE,)),
            dma((PLANE,)),
            dma((PLANE,)),
            dma((PLANE,)),
            dma((planes,)),
            dma((planes,)),
            dma((PLANE,)),
            dma((PLANE,)),
            dma((cols,)),
            dma((cols,)),
            dma((nm,)),
            dma((nm,)),
            dma((nm,)),
            dma((nm,)),
            dma((PLANE,)),
            dma((PLANE,)),
            dma((PLANE,)),
            dma((PLANE,)),
        ],
        compiler_params=pltpu.CompilerParams(
            collective_id=0, has_side_effects=True, vmem_limit_bytes=56 * 2**20
        ),
    )(kernel, basis_t, responses)


def local(kernel, basis, responses):
    return tuple(step(kernel, basis.T, responses))


def solution(mesh):
    return jax.shard_map(
        local,
        mesh=mesh,
        in_specs=(P("row", "col"), P("col", "row"), P("row", "col")),
        out_specs=(
            P("row", None),
            P("row", "col"),
            P("col", None),
            P("row", "col"),
            P("row", None),
        ),
        check_vma=False,
    )
```

```python
import math

import jax
import jax.numpy as jnp
from jax import lax
from jax.experimental import pallas as pl
from jax.experimental.pallas import tpu as pltpu
from jax.sharding import PartitionSpec as P

MESH = pl.DeviceIdType.MESH
HIGHEST = lax.Precision.HIGHEST
PLANE = 4
LAST = (((1,), (1,)), ((), ()))
FIRST = (((0,), (0,)), ((), ()))
PLAIN = (((1,), (0,)), ((), ()))


def dot(a, b, dims):
    return lax.dot_general(a, b, dims, precision=HIGHEST, preferred_element_type=jnp.float32)


def chunks_of(width, most):
    return max(c for c in range(1, most + 1) if width % (c * 128) == 0)


def remote(src, dst, send, recv, device):
    return pltpu.make_async_remote_copy(
        src_ref=src,
        dst_ref=dst,
        send_sem=send,
        recv_sem=recv,
        device_id=device,
        device_id_type=MESH,
    )


def done(ref, sem):
    pltpu.make_async_copy(ref, ref, sem).wait()


def inverse_factor(work, inverse, comp):
    lane = lax.broadcasted_iota(jnp.int32, (8, comp), 1)
    sub = lax.broadcasted_iota(jnp.int32, (8, 1), 0)

    def panel(p, carry):
        top = pl.multiple_of(p * 8, 8)
        left = work[pl.ds(top, 8), :comp]
        right = work[pl.ds(top, 8), comp:]
        cols = [
            jnp.sum(jnp.where(lane == top + j, left, 0.0), axis=1, keepdims=True) for j in range(8)
        ]
        for j in range(8):
            scale = 1.0 / jnp.sqrt(cols[j][j : j + 1, :])
            mult = jnp.where(sub > j, cols[j] * scale, 0.0)
            left_row = left[j : j + 1, :] * scale
            right_row = right[j : j + 1, :] * scale
            left = jnp.where(sub == j, left_row, left - mult * left_row)
            right = jnp.where(sub == j, right_row, right - mult * right_row)
            for m in range(j + 1, 8):
                cols[m] = cols[m] - mult * (cols[m][j : j + 1, :] * scale)
        inverse[pl.ds(top, 8), :] = right
        work[...] = work[...] - dot(left, jnp.concatenate([left, right], axis=1), FIRST)
        return carry

    lax.fori_loop(0, comp // 8, panel, 0)


def step(kernel, basis_t, responses):
    n, cols = lax.axis_size("row"), lax.axis_size("col")
    planes = n // PLANE
    height, total = kernel.shape
    here = basis_t.shape[0]
    comp = here * n
    resp = responses.shape[1]
    width = total // PLANE
    rows = height * PLANE
    group = PLANE * cols
    slab = rows // group
    gram_slab = comp // PLANE
    resp_slab = resp // PLANE
    root_rows = math.sqrt(height * n)
    root_resp = math.sqrt(resp * cols)
    nk = chunks_of(width, 8)
    wk = width // nk
    nm = chunks_of(width, 32)
    wm = width // nm
    ahead_k, ahead_b = min(2, nk), min(2, nk)
    half = planes // 2

    def body(
        k_hbm,
        b_hbm,
        resp_ref,
        scores,
        loadings,
        weights,
        deflated,
        nxt,
        kx,
        bq,
        acc,
        outer,
        tot,
        lbuf,
        part,
        part_in,
        full,
        full_t,
        gram,
        gram_in,
        gram_sum,
        gram_full,
        work,
        inverse,
        mix,
        t_own,
        t_in,
        t_sum,
        t_z,
        t_full,
        next_own,
        next_in,
        k_send,
        k_recv,
        b_send,
        b_recv,
        zb_send,
        zb_recv,
        p_send,
        p_recv,
        f_send,
        f_recv,
        g_send,
        g_recv,
        gf_send,
        gf_recv,
        t_send,
        t_recv,
        tz_send,
        tz_recv,
        tf_send,
        tf_recv,
        n_send,
        n_recv,
        in_send,
        in_recv,
        tot_send,
        tot_recv,
        d_send,
        d_recv,
        l_send,
        l_recv,
    ):
        me, col = lax.axis_index("row"), lax.axis_index("col")
        z, q = me // PLANE, me % PLANE
        y, x = q // 2, q % 2

        def peer(k):
            return (1 - y if k & 2 else y) * 2 + (1 - x if k & 1 else x)

        peers = [peer(k) for k in range(PLANE)]
        mine = q * cols + col

        def member(d):
            other = lax.rem(mine + d, group)
            return other, {"row": z * PLANE + other // cols, "col": other % cols}

        def plane_of(d):
            return lax.rem(z + d, planes)

        def above(f):
            pl.when(z < planes - 1)(f)

        def below(f):
            pl.when(z > 0)(f)

        def span(c, w):
            return pl.ds(pl.multiple_of(c * w, w), w)

        def quarter(k, c, w):
            return pl.ds(pl.multiple_of(peers[k] * width + c * w, w), w)

        def k_copy(c, k):
            src = k_hbm.at[:, quarter(k, c, wk)]
            dst = kx.at[q, :, span(c, wk)]
            if k == 0:
                return pltpu.make_async_copy(src, dst, k_recv.at[c, 0])
            return remote(
                src, dst, k_send.at[k], k_recv.at[c, k], {"row": z * PLANE + peers[k]}
            )

        def b_copy(c, k):
            src = b_hbm.at[:, quarter(k, c, wk)]
            dst = bq.at[me, :, span(c, wk)]
            if k == 0:
                return pltpu.make_async_copy(src, dst, b_recv.at[c, 0])
            return remote(
                src, dst, b_send.at[k], b_recv.at[c, k], {"row": z * PLANE + peers[k]}
            )

        def bz_block(c, origin):
            return bq.at[pl.ds(origin * PLANE, PLANE), :, span(c, wk)]

        def bz_copy(c, origin, way):
            ref = bz_block(c, origin)
            return remote(
                ref,
                ref,
                zb_send.at[(way + 1) // 2, c, origin],
                zb_recv.at[c, origin],
                {"row": me + way * PLANE},
            )

        def bz_first(c):
            for k in range(PLANE):
                done(bq.at[z * PLANE + peers[k], :, span(c, wk)], b_recv.at[c, k])

            @above
            def _():
                bz_copy(c, z, 1).start()

            @below
            def _():
                bz_copy(c, z, -1).start()

        def bz_relay(c):
            for d in range(1, planes):

                @pl.when(z - d >= 0)
                def _(d=d):
                    done(bz_block(c, z - d), zb_recv.at[c, z - d])

                    @above
                    def _():
                        bz_copy(c, z - d, 1).start()

                @pl.when(z + d < planes)
                def _(d=d):
                    done(bz_block(c, z + d), zb_recv.at[c, z + d])

                    @below
                    def _():
                        bz_copy(c, z + d, -1).start()

        b_own = [b_copy(c, 0) for c in range(nk)]
        for copy in b_own:
            copy.start()

        def k_own(c, carry):
            k_copy(c, 0).start()
            return carry

        lax.fori_loop(0, nk, k_own, 0)

        barrier = pltpu.get_barrier_semaphore()
        for d in range(1, group):
            pl.semaphore_signal(barrier, inc=1, device_id=member(d)[1], device_id_type=MESH)
        for d in range(1, planes):
            pl.semaphore_signal(
                barrier,
                inc=1,
                device_id={"row": plane_of(d) * PLANE + q},
                device_id_type=MESH,
            )
        pl.semaphore_wait(barrier, group + planes - 2)

        def b_start(c, carry):
            for k in range(1, PLANE):
                b_copy(c, k).start()
            return carry

        lax.fori_loop(0, nk, b_start, 0)
        for c in range(ahead_k):
            for k in range(1, PLANE):
                k_copy(c, k).start()
        for c in range(ahead_b):
            bz_first(c)
        part[...] = jnp.zeros_like(part)

        def project(c, carry):
            @pl.when(c + ahead_k < nk)
            def _():
                for k in range(1, PLANE):
                    k_copy(c + ahead_k, k).start()

            @pl.when(c + ahead_b < nk)
            def _():
                bz_first(c + ahead_b)

            bz_relay(c)
            for k in range(PLANE):
                done(kx.at[peers[k], :, span(c, wk)], k_recv.at[c, k])
            here_k = kx[:, :, span(c, wk)].reshape(rows, wk)
            here_b = bq[:, :, span(c, wk)].reshape(comp, wk)
            part[...] += dot(here_k, here_b, LAST).reshape(part.shape)
            return carry

        lax.fori_loop(0, nk, project, 0)

        for d in range(1, group):
            other, device = member(d)
            remote(
                part.at[other], part_in.at[mine], p_send.at[other], p_recv.at[mine], device
            ).start()
        total_rows = part[mine]
        for d in range(1, group):
            other, _ = member(d)
            done(part_in.at[other], p_recv.at[other])
            total_rows = total_rows + part_in[other]
        full[mine] = total_rows
        for d in range(1, group):
            other, device = member(d)
            remote(
                full.at[mine], full.at[mine], f_send.at[other], f_recv.at[mine], device
            ).start()
        for d in range(1, group):
            other, _ = member(d)
            done(full.at[other], f_recv.at[other])
        projected = full[...].reshape(rows, comp)

        gram[...] = dot(projected, projected, FIRST).reshape(gram.shape)

        def g_copy(d):
            return remote(
                gram.at[q],
                gram_in.at[z],
                g_send.at[plane_of(d)],
                g_recv.at[z],
                {"row": plane_of(d) * PLANE + q},
            )

        for d in range(1, planes):
            g_copy(d).start()
        gram_in[z] = gram[q]
        full_t[...] = projected.T

        lower = z < half
        inner_z = jnp.where(lower, z + 1, z - 1)
        outer_z = jnp.where(lower, z - 1, z + 1)
        centre = jnp.logical_or(z == half - 1, z == half)
        inward = {"row": inner_z * PLANE + q}
        outward = {"row": outer_z * PLANE + q}
        has_outer = jnp.logical_and(z > 0, z < planes - 1)

        def in_copy(c, to, recv):
            return remote(
                acc.at[:, span(c, wm)], to.at[:, span(c, wm)], in_send.at[c], recv.at[c], inward
            )

        def tot_copy(c):
            ref = tot.at[:, span(c, wm)]
            return remote(ref, ref, tot_send.at[c], tot_recv.at[c], outward)

        def gather_in(c):
            own = dot(full_t[...], kx[:, :, span(c, wm)].reshape(rows, wm), PLAIN)
            acc[:, span(c, wm)] = own

            @pl.when(has_outer)
            def _():
                done(outer.at[:, span(c, wm)], in_recv.at[c])
                acc[:, span(c, wm)] = acc[:, span(c, wm)] + outer[:, span(c, wm)]

            @pl.when(centre)
            def _():
                in_copy(c, tot, tot_recv).start()

            @pl.when(jnp.logical_not(centre))
            def _():
                in_copy(c, outer, in_recv).start()

        hops = jnp.where(lower, half - 1 - z, z - half)
        early = jnp.minimum(hops * 4, nm)
        ahead_m = jnp.minimum(3 + hops * 4, nm)

        def gather_some(first, last):
            def one(c, carry):
                gather_in(c)
                return carry

            lax.fori_loop(first, last, one, 0)

        gather_some(0, early)

        for d in range(1, planes):
            done(gram_in.at[plane_of(d)], g_recv.at[plane_of(d)])
        gram_full[q] = jnp.sum(gram_in[...], axis=0)

        def gf_copy(k):
            return remote(
                gram_full.at[q],
                gram_full.at[q],
                gf_send.at[k],
                gf_recv.at[k],
                {"row": z * PLANE + peers[k]},
            )

        for k in range(1, PLANE):
            gf_copy(k).start()

        own_rows = full[pl.ds(q * cols, cols)].reshape(height, comp)
        t_own[...] = dot(resp_ref[...], own_rows, FIRST).reshape(t_own.shape)
        for k in range(1, PLANE):
            remote(
                t_own.at[peers[k]],
                t_in.at[q],
                t_send.at[k],
                t_recv.at[k],
                {"row": z * PLANE + peers[k]},
            ).start()
        t_in[q] = t_own[q]
        first = jnp.maximum(early, 1)
        gather_some(early, first)
        for k in range(1, PLANE):
            done(gram_full.at[peers[k]], gf_recv.at[k])
        work[:, :comp] = gram_full[...].reshape(comp, comp) * (1.0 / (height * n))
        work[:, comp:] = (
            lax.broadcasted_iota(jnp.int32, (comp, comp), 0)
            == lax.broadcasted_iota(jnp.int32, (comp, comp), 1)
        ).astype(jnp.float32)
        inverse_factor(work, inverse, comp)
        plane_scores = dot(projected, inverse[...], LAST)
        mix[pl.ds(0, rows), :] = dot(plane_scores, inverse[...], PLAIN) * (1.0 / (height * n))
        mix[pl.ds(rows, here * PLANE), :] = inverse[
            pl.ds(pl.multiple_of(z * (here * PLANE), here * PLANE), here * PLANE), :
        ] * (1.0 / root_rows)
        scores[...] = dot(own_rows, inverse[...], LAST)

        for k in range(1, PLANE):
            done(t_in.at[peers[k]], t_recv.at[k])
        t_z[z] = jnp.sum(t_in[...], axis=0)
        t_sum[...] = t_z[z]
        for d in range(1, planes):
            remote(
                t_sum,
                t_z.at[z],
                tz_send.at[plane_of(d)],
                tz_recv.at[z],
                {"row": plane_of(d) * PLANE + q},
            ).start()

        gather_some(first, ahead_m)

        def d_copy(c, k):
            src = kx.at[peers[k], :, span(c, wm)]
            dst = deflated.at[:, quarter(0, c, wm)]
            if k == 0:
                return pltpu.make_async_copy(src, dst, d_recv.at[0])
            return remote(src, dst, d_send.at[k], d_recv.at[k], {"row": z * PLANE + peers[k]})

        def l_copy(c, k):
            src = lbuf.at[peers[k], :, span(c, wm)]
            dst = loadings.at[:, quarter(0, c, wm)]
            if k == 0:
                return pltpu.make_async_copy(src, dst, l_recv.at[0])
            return remote(src, dst, l_send.at[k], l_recv.at[k], {"row": z * PLANE + peers[k]})

        def deflate(c, carry):
            @pl.when(c + ahead_m < nm)
            def _():
                gather_in(c + ahead_m)

            done(tot.at[:, span(c, wm)], tot_recv.at[c])

            @pl.when(centre)
            def _():
                tot[:, span(c, wm)] = tot[:, span(c, wm)] + acc[:, span(c, wm)]

            @pl.when(has_outer)
            def _():
                tot_copy(c).start()

            product = dot(mix[...], tot[:, span(c, wm)], PLAIN)
            kx[:, :, span(c, wm)] = kx[:, :, span(c, wm)] - product[:rows].reshape(
                PLANE, height, wm
            )
            lbuf[:, :, span(c, wm)] = product[rows:].reshape(PLANE, here, wm)
            for k in (3, 1, 2, 0):
                d_copy(c, k).start()
                l_copy(c, k).start()
            return carry

        lax.fori_loop(0, nm, deflate, 0)

        for d in range(1, planes):
            done(t_z.at[plane_of(d)], tz_recv.at[plane_of(d)])
        t_full[q] = jnp.sum(t_z[...], axis=0)
        for k in range(1, PLANE):
            remote(
                t_full.at[q],
                t_full.at[q],
                tf_send.at[k],
                tf_recv.at[k],
                {"row": z * PLANE + peers[k]},
            ).start()
        for k in range(1, PLANE):
            done(t_full.at[peers[k]], tf_recv.at[k])
        weights_here = dot(t_full[...].reshape(resp, comp), inverse[...], LAST) * (1.0 / root_rows)
        weights[...] = weights_here
        next_own[...] = dot(resp_ref[...], weights_here, PLAIN) * (1.0 / root_resp)
        next_in[col] = next_own[...]
        for d in range(1, cols):
            there = lax.rem(col + d, cols)
            remote(
                next_own, next_in.at[col], n_send.at[there], n_recv.at[col], {"col": there}
            ).start()
        for d in range(1, cols):
            there = lax.rem(col + d, cols)
            done(next_in.at[there], n_recv.at[there])
        nxt[...] = jnp.sum(next_in[...], axis=0)

        for k in range(PLANE):
            done(deflated.at[:, pl.ds(pl.multiple_of(peers[k] * width, width), width)], d_recv.at[k])
            done(loadings.at[:, pl.ds(pl.multiple_of(peers[k] * width, width), width)], l_recv.at[k])
        for k in range(1, PLANE):
            done(kx.at[0], k_send.at[k])
            done(bq.at[0], b_send.at[k])
            done(kx.at[0], d_send.at[k])
            done(lbuf.at[0], l_send.at[k])
            done(t_own.at[0], t_send.at[k])
            done(t_full.at[0], tf_send.at[k])
            done(gram_full.at[0], gf_send.at[k])
        for d in range(1, group):
            other, _ = member(d)
            done(part.at[0], p_send.at[other])
            done(full.at[0], f_send.at[other])
        for d in range(1, planes):
            done(gram.at[0], g_send.at[plane_of(d)])
            done(t_sum, tz_send.at[plane_of(d)])
        for d in range(1, cols):
            done(next_own, n_send.at[lax.rem(col + d, cols)])

        def b_end(c, carry):
            for o in range(planes):

                @pl.when(jnp.logical_and(z < planes - 1, o <= z))
                def _(o=o):
                    done(bz_block(c, o), zb_send.at[1, c, o])

                @pl.when(jnp.logical_and(z > 0, o >= z))
                def _(o=o):
                    done(bz_block(c, o), zb_send.at[0, c, o])

            return carry

        lax.fori_loop(0, nk, b_end, 0)

        def m_end(c, carry):
            done(acc.at[:, span(c, wm)], in_send.at[c])

            @pl.when(has_outer)
            def _():
                done(tot.at[:, span(c, wm)], tot_send.at[c])

            return carry

        lax.fori_loop(0, nm, m_end, 0)

    f32 = jnp.float32
    dma = pltpu.SemaphoreType.DMA
    vmem = pl.BlockSpec(memory_space=pltpu.VMEM)
    hbm = pl.BlockSpec(memory_space=pltpu.HBM)
    anywhere = pl.BlockSpec(memory_space=pl.ANY)
    return pl.pallas_call(
        body,
        out_shape=[
            pltpu.VMEM((height, comp), f32),
            pltpu.VMEM((here, total), f32),
            pltpu.VMEM((resp, comp), f32),
            pltpu.VMEM((height, total), f32),
            pltpu.VMEM((height, comp), f32),
        ],
        in_specs=[hbm, hbm, vmem],
        out_specs=[vmem, anywhere, vmem, anywhere, vmem],
        scratch_shapes=[
            pltpu.VMEM((PLANE, height, width), f32),
            pltpu.VMEM((n, here, width), f32),
            pltpu.VMEM((comp, width), f32),
            pltpu.VMEM((comp, width), f32),
            pltpu.VMEM((comp, width), f32),
            pltpu.VMEM((PLANE, here, width), f32),
            pltpu.VMEM((group, slab, comp), f32),
            pltpu.VMEM((group, slab, comp), f32),
            pltpu.VMEM((group, slab, comp), f32),
            pltpu.VMEM((comp, rows), f32),
            pltpu.VMEM((PLANE, gram_slab, comp), f32),
            pltpu.VMEM((planes, gram_slab, comp), f32),
            pltpu.VMEM((gram_slab, comp), f32),
            pltpu.VMEM((PLANE, gram_slab, comp), f32),
            pltpu.VMEM((comp, 2 * comp), f32),
            pltpu.VMEM((comp, comp), f32),
            pltpu.VMEM((rows + here * PLANE, comp), f32),
            pltpu.VMEM((PLANE, resp_slab, comp), f32),
            pltpu.VMEM((PLANE, resp_slab, comp), f32),
            pltpu.VMEM((resp_slab, comp), f32),
            pltpu.VMEM((planes, resp_slab, comp), f32),
            pltpu.VMEM((PLANE, resp_slab, comp), f32),
            pltpu.VMEM((height, comp), f32),
            pltpu.VMEM((cols, height, comp), f32),
            dma((PLANE,)),
            dma((nk, PLANE)),
            dma((PLANE,)),
            dma((nk, PLANE)),
            dma((2, nk, planes)),
            dma((nk, planes)),
            dma((group,)),
            dma((group,)),
            dma((group,)),
            dma((group,)),
            dma((planes,)),
            dma((planes,)),
            dma((PLANE,)),
            dma((PLANE,)),
            dma((PLANE,)),
            dma((PLANE,)),
            dma((planes,)),
            dma((planes,)),
            dma((PLANE,)),
            dma((PLANE,)),
            dma((cols,)),
            dma((cols,)),
            dma((nm,)),
            dma((nm,)),
            dma((nm,)),
            dma((nm,)),
            dma((PLANE,)),
            dma((PLANE,)),
            dma((PLANE,)),
            dma((PLANE,)),
        ],
        compiler_params=pltpu.CompilerParams(
            collective_id=0, has_side_effects=True, vmem_limit_bytes=40 * 2**20
        ),
    )(kernel, basis_t, responses)


def hand_over(arrays):
    pieces = [(i, r) for i, a in enumerate(arrays) for r in range(0, a.shape[0], 8 if a.size > 2**18 else a.shape[0])]

    def body(*refs):
        count = len(arrays)
        sems = refs[-1]
        copies = []
        for j, (i, r) in enumerate(pieces):
            rows = pl.ds(r, 8 if arrays[i].size > 2**18 else arrays[i].shape[0])
            copies.append(
                pltpu.make_async_copy(refs[i].at[rows], refs[count + i].at[rows], sems.at[j])
            )
        for copy in copies:
            copy.start()
        for copy in copies:
            copy.wait()

    anywhere = pl.BlockSpec(memory_space=pl.ANY)
    return pl.pallas_call(
        body,
        out_shape=[jax.ShapeDtypeStruct(a.shape, a.dtype) for a in arrays],
        in_specs=[pl.BlockSpec(memory_space=pltpu.VMEM)] * len(arrays),
        out_specs=[anywhere] * len(arrays),
        scratch_shapes=[pltpu.SemaphoreType.DMA((len(pieces),))],
        compiler_params=pltpu.CompilerParams(vmem_limit_bytes=2**20),
    )(*arrays)


def local(kernel, basis, responses):
    return tuple(hand_over(step(kernel, basis.T, responses)))


def solution(mesh):
    return jax.shard_map(
        local,
        mesh=mesh,
        in_specs=(P("row", "col"), P("col", "row"), P("row", "col")),
        out_specs=(
            P("row", None),
            P("row", "col"),
            P("col", None),
            P("row", "col"),
            P("row", None),
        ),
        check_vma=False,
    )
```

```python
import math

import jax
import jax.numpy as jnp
from jax import lax
from jax.experimental import pallas as pl
from jax.experimental.pallas import tpu as pltpu
from jax.sharding import PartitionSpec as P

MESH = pl.DeviceIdType.MESH
HIGHEST = lax.Precision.HIGHEST
PLANE = 4
LAST = (((1,), (1,)), ((), ()))
FIRST = (((0,), (0,)), ((), ()))
PLAIN = (((1,), (0,)), ((), ()))


def dot(a, b, dims):
    return lax.dot_general(a, b, dims, precision=HIGHEST, preferred_element_type=jnp.float32)


def chunks_of(width, most):
    return max(c for c in range(1, most + 1) if width % (c * 128) == 0)


def remote(src, dst, send, recv, device):
    return pltpu.make_async_remote_copy(
        src_ref=src,
        dst_ref=dst,
        send_sem=send,
        recv_sem=recv,
        device_id=device,
        device_id_type=MESH,
    )


def done(ref, sem):
    pltpu.make_async_copy(ref, ref, sem).wait()


def inverse_factor(work, inverse, comp, between):
    lane = lax.broadcasted_iota(jnp.int32, (8, comp), 1)
    sub = lax.broadcasted_iota(jnp.int32, (8, 1), 0)

    def panel(p, carry):
        top = pl.multiple_of(p * 8, 8)
        left = work[pl.ds(top, 8), :comp]
        right = work[pl.ds(top, 8), comp:]
        cols = [
            jnp.sum(jnp.where(lane == top + j, left, 0.0), axis=1, keepdims=True) for j in range(8)
        ]
        for j in range(8):
            scale = 1.0 / jnp.sqrt(cols[j][j : j + 1, :])
            mult = jnp.where(sub > j, cols[j] * scale, 0.0)
            left_row = left[j : j + 1, :] * scale
            right_row = right[j : j + 1, :] * scale
            left = jnp.where(sub == j, left_row, left - mult * left_row)
            right = jnp.where(sub == j, right_row, right - mult * right_row)
            for m in range(j + 1, 8):
                cols[m] = cols[m] - mult * (cols[m][j : j + 1, :] * scale)
        inverse[pl.ds(top, 8), :] = right
        work[...] = work[...] - dot(left, jnp.concatenate([left, right], axis=1), FIRST)
        between(p)
        return carry

    lax.fori_loop(0, comp // 8, panel, 0)


def step(kernel, basis_t, responses):
    n, cols = lax.axis_size("row"), lax.axis_size("col")
    planes = n // PLANE
    height, total = kernel.shape
    here = basis_t.shape[0]
    comp = here * n
    resp = responses.shape[1]
    width = total // PLANE
    rows = height * PLANE
    group = PLANE * cols
    slab = rows // group
    gram_slab = comp // PLANE
    resp_slab = resp // PLANE
    root_rows = math.sqrt(height * n)
    root_resp = math.sqrt(resp * cols)
    nk = chunks_of(width, 8)
    wk = width // nk
    nm = chunks_of(width, 32)
    wm = width // nm
    ahead_k, ahead_b = min(2, nk), min(2, nk)
    every = 8
    turns = comp // 8 // every
    half = planes // 2

    def body(
        k_hbm,
        b_hbm,
        resp_ref,
        scores,
        loadings,
        weights,
        deflated,
        nxt,
        kx,
        bq,
        acc,
        outer,
        tot,
        lbuf,
        part,
        part_in,
        full,
        full_t,
        gram,
        gram_in,
        gram_sum,
        gram_full,
        work,
        inverse,
        mix,
        t_own,
        t_in,
        t_sum,
        t_z,
        t_full,
        next_own,
        next_in,
        k_send,
        k_recv,
        b_send,
        b_recv,
        zb_send,
        zb_recv,
        p_send,
        p_recv,
        f_send,
        f_recv,
        g_send,
        g_recv,
        gf_send,
        gf_recv,
        t_send,
        t_recv,
        tz_send,
        tz_recv,
        tf_send,
        tf_recv,
        n_send,
        n_recv,
        in_send,
        in_recv,
        tot_send,
        tot_recv,
        d_send,
        d_recv,
        l_send,
        l_recv,
    ):
        me, col = lax.axis_index("row"), lax.axis_index("col")
        z, q = me // PLANE, me % PLANE
        y, x = q // 2, q % 2

        def peer(k):
            return (1 - y if k & 2 else y) * 2 + (1 - x if k & 1 else x)

        peers = [peer(k) for k in range(PLANE)]
        mine = q * cols + col

        def member(d):
            other = lax.rem(mine + d, group)
            return other, {"row": z * PLANE + other // cols, "col": other % cols}

        def plane_of(d):
            return lax.rem(z + d, planes)

        def above(f):
            pl.when(z < planes - 1)(f)

        def below(f):
            pl.when(z > 0)(f)

        def span(c, w):
            return pl.ds(pl.multiple_of(c * w, w), w)

        def quarter(k, c, w):
            return pl.ds(pl.multiple_of(peers[k] * width + c * w, w), w)

        def k_copy(c, k):
            src = k_hbm.at[:, quarter(k, c, wk)]
            dst = kx.at[q, :, span(c, wk)]
            if k == 0:
                return pltpu.make_async_copy(src, dst, k_recv.at[c, 0])
            return remote(
                src, dst, k_send.at[k], k_recv.at[c, k], {"row": z * PLANE + peers[k]}
            )

        def b_copy(c, k):
            src = b_hbm.at[:, quarter(k, c, wk)]
            dst = bq.at[me, :, span(c, wk)]
            if k == 0:
                return pltpu.make_async_copy(src, dst, b_recv.at[c, 0])
            return remote(
                src, dst, b_send.at[k], b_recv.at[c, k], {"row": z * PLANE + peers[k]}
            )

        def bz_block(c, origin):
            return bq.at[pl.ds(origin * PLANE, PLANE), :, span(c, wk)]

        def bz_copy(c, origin, way):
            ref = bz_block(c, origin)
            return remote(
                ref,
                ref,
                zb_send.at[(way + 1) // 2, c, origin],
                zb_recv.at[c, origin],
                {"row": me + way * PLANE},
            )

        def bz_first(c):
            for k in range(PLANE):
                done(bq.at[z * PLANE + peers[k], :, span(c, wk)], b_recv.at[c, k])

            @above
            def _():
                bz_copy(c, z, 1).start()

            @below
            def _():
                bz_copy(c, z, -1).start()

        def bz_relay(c):
            for d in range(1, planes):

                @pl.when(z - d >= 0)
                def _(d=d):
                    done(bz_block(c, z - d), zb_recv.at[c, z - d])

                    @above
                    def _():
                        bz_copy(c, z - d, 1).start()

                @pl.when(z + d < planes)
                def _(d=d):
                    done(bz_block(c, z + d), zb_recv.at[c, z + d])

                    @below
                    def _():
                        bz_copy(c, z + d, -1).start()

        b_own = [b_copy(c, 0) for c in range(nk)]
        for copy in b_own:
            copy.start()

        def k_own(c, carry):
            k_copy(c, 0).start()
            return carry

        lax.fori_loop(0, nk, k_own, 0)

        barrier = pltpu.get_barrier_semaphore()
        for d in range(1, group):
            pl.semaphore_signal(barrier, inc=1, device_id=member(d)[1], device_id_type=MESH)
        for d in range(1, planes):
            pl.semaphore_signal(
                barrier,
                inc=1,
                device_id={"row": plane_of(d) * PLANE + q},
                device_id_type=MESH,
            )
        pl.semaphore_wait(barrier, group + planes - 2)

        def b_start(c, carry):
            for k in range(1, PLANE):
                b_copy(c, k).start()
            return carry

        lax.fori_loop(0, nk, b_start, 0)
        for c in range(ahead_k):
            for k in range(1, PLANE):
                k_copy(c, k).start()
        for c in range(ahead_b):
            bz_first(c)
        part[...] = jnp.zeros_like(part)

        def project(c, carry):
            @pl.when(c + ahead_k < nk)
            def _():
                for k in range(1, PLANE):
                    k_copy(c + ahead_k, k).start()

            @pl.when(c + ahead_b < nk)
            def _():
                bz_first(c + ahead_b)

            bz_relay(c)
            for k in range(PLANE):
                done(kx.at[peers[k], :, span(c, wk)], k_recv.at[c, k])
            here_k = kx[:, :, span(c, wk)].reshape(rows, wk)
            here_b = bq[:, :, span(c, wk)].reshape(comp, wk)
            part[...] += dot(here_k, here_b, LAST).reshape(part.shape)
            return carry

        lax.fori_loop(0, nk, project, 0)

        for d in range(1, group):
            other, device = member(d)
            remote(
                part.at[other], part_in.at[mine], p_send.at[other], p_recv.at[mine], device
            ).start()
        total_rows = part[mine]
        for d in range(1, group):
            other, _ = member(d)
            done(part_in.at[other], p_recv.at[other])
            total_rows = total_rows + part_in[other]
        full[mine] = total_rows
        for d in range(1, group):
            other, device = member(d)
            remote(
                full.at[mine], full.at[mine], f_send.at[other], f_recv.at[mine], device
            ).start()
        for d in range(1, group):
            other, _ = member(d)
            done(full.at[other], f_recv.at[other])
        projected = full[...].reshape(rows, comp)

        gram[...] = dot(projected, projected, FIRST).reshape(gram.shape)

        def g_copy(d):
            return remote(
                gram.at[q],
                gram_in.at[z],
                g_send.at[plane_of(d)],
                g_recv.at[z],
                {"row": plane_of(d) * PLANE + q},
            )

        for d in range(1, planes):
            g_copy(d).start()
        gram_in[z] = gram[q]
        full_t[...] = projected.T

        lower = z < half
        inner_z = jnp.where(lower, z + 1, z - 1)
        outer_z = jnp.where(lower, z - 1, z + 1)
        centre = jnp.logical_or(z == half - 1, z == half)
        inward = {"row": inner_z * PLANE + q}
        outward = {"row": outer_z * PLANE + q}
        has_outer = jnp.logical_and(z > 0, z < planes - 1)

        def in_copy(c, to, recv):
            return remote(
                acc.at[:, span(c, wm)], to.at[:, span(c, wm)], in_send.at[c], recv.at[c], inward
            )

        def tot_copy(c):
            ref = tot.at[:, span(c, wm)]
            return remote(ref, ref, tot_send.at[c], tot_recv.at[c], outward)

        def gather_in(c):
            own = dot(full_t[...], kx[:, :, span(c, wm)].reshape(rows, wm), PLAIN)
            acc[:, span(c, wm)] = own

            @pl.when(has_outer)
            def _():
                done(outer.at[:, span(c, wm)], in_recv.at[c])
                acc[:, span(c, wm)] = acc[:, span(c, wm)] + outer[:, span(c, wm)]

            @pl.when(centre)
            def _():
                in_copy(c, tot, tot_recv).start()

            @pl.when(jnp.logical_not(centre))
            def _():
                in_copy(c, outer, in_recv).start()

        hops = jnp.where(lower, half - 1 - z, z - half)
        early = jnp.minimum(hops * 4, nm)
        ahead_m = jnp.minimum(turns + 1 + hops * 6, nm)

        def finish(c):
            done(tot.at[:, span(c, wm)], tot_recv.at[c])

            @pl.when(centre)
            def _():
                tot[:, span(c, wm)] = tot[:, span(c, wm)] + acc[:, span(c, wm)]

            @pl.when(has_outer)
            def _():
                tot_copy(c).start()

        def gather_some(first, last):
            def one(c, carry):
                gather_in(c)
                return carry

            lax.fori_loop(first, last, one, 0)

        gather_some(0, early)

        for d in range(1, planes):
            done(gram_in.at[plane_of(d)], g_recv.at[plane_of(d)])
        gram_full[q] = jnp.sum(gram_in[...], axis=0)

        def gf_copy(k):
            return remote(
                gram_full.at[q],
                gram_full.at[q],
                gf_send.at[k],
                gf_recv.at[k],
                {"row": z * PLANE + peers[k]},
            )

        for k in range(1, PLANE):
            gf_copy(k).start()

        own_rows = full[pl.ds(q * cols, cols)].reshape(height, comp)
        t_own[...] = dot(resp_ref[...], own_rows, FIRST).reshape(t_own.shape)
        for k in range(1, PLANE):
            remote(
                t_own.at[peers[k]],
                t_in.at[q],
                t_send.at[k],
                t_recv.at[k],
                {"row": z * PLANE + peers[k]},
            ).start()
        t_in[q] = t_own[q]
        first = jnp.maximum(early, 1)
        gather_some(early, first)
        for k in range(1, PLANE):
            done(gram_full.at[peers[k]], gf_recv.at[k])
        work[:, :comp] = gram_full[...].reshape(comp, comp) * (1.0 / (height * n))
        work[:, comp:] = (
            lax.broadcasted_iota(jnp.int32, (comp, comp), 0)
            == lax.broadcasted_iota(jnp.int32, (comp, comp), 1)
        ).astype(jnp.float32)

        def between(p):
            turn = p // every

            @pl.when(jnp.logical_and(p % every == every - 1, first + turn < nm))
            def _():
                gather_in(first + turn)

            @pl.when(jnp.logical_and(centre, jnp.logical_and(p % every == every - 1, turn > 0)))
            def _():
                finish(turn - 1)

        inverse_factor(work, inverse, comp, between)
        plane_scores = dot(projected, inverse[...], LAST)
        mix[pl.ds(0, rows), :] = dot(plane_scores, inverse[...], PLAIN) * (1.0 / (height * n))
        mix[pl.ds(rows, here * PLANE), :] = inverse[
            pl.ds(pl.multiple_of(z * (here * PLANE), here * PLANE), here * PLANE), :
        ] * (1.0 / root_rows)
        scores[...] = dot(own_rows, inverse[...], LAST)

        for k in range(1, PLANE):
            done(t_in.at[peers[k]], t_recv.at[k])
        t_z[z] = jnp.sum(t_in[...], axis=0)
        t_sum[...] = t_z[z]
        for d in range(1, planes):
            remote(
                t_sum,
                t_z.at[z],
                tz_send.at[plane_of(d)],
                tz_recv.at[z],
                {"row": plane_of(d) * PLANE + q},
            ).start()

        gather_some(jnp.minimum(first + turns, nm), ahead_m)

        def d_copy(c, k):
            src = kx.at[peers[k], :, span(c, wm)]
            dst = deflated.at[:, quarter(0, c, wm)]
            if k == 0:
                return pltpu.make_async_copy(src, dst, d_recv.at[0])
            return remote(src, dst, d_send.at[k], d_recv.at[k], {"row": z * PLANE + peers[k]})

        def l_copy(c, k):
            src = lbuf.at[peers[k], :, span(c, wm)]
            dst = loadings.at[:, quarter(0, c, wm)]
            if k == 0:
                return pltpu.make_async_copy(src, dst, l_recv.at[0])
            return remote(src, dst, l_send.at[k], l_recv.at[k], {"row": z * PLANE + peers[k]})

        def sum_responses():
            for d in range(1, planes):
                done(t_z.at[plane_of(d)], tz_recv.at[plane_of(d)])
            t_full[q] = jnp.sum(t_z[...], axis=0)
            for k in range(1, PLANE):
                remote(
                    t_full.at[q],
                    t_full.at[q],
                    tf_send.at[k],
                    tf_recv.at[k],
                    {"row": z * PLANE + peers[k]},
                ).start()

        def weigh():
            for k in range(1, PLANE):
                done(t_full.at[peers[k]], tf_recv.at[k])
            weights_here = dot(t_full[...].reshape(resp, comp), inverse[...], LAST) * (1.0 / root_rows)
            weights[...] = weights_here
            next_own[...] = dot(resp_ref[...], weights_here, PLAIN) * (1.0 / root_resp)
            next_in[col] = next_own[...]
            for d in range(1, cols):
                there = lax.rem(col + d, cols)
                remote(
                    next_own, next_in.at[col], n_send.at[there], n_recv.at[col], {"col": there}
                ).start()

        def deflate(c, carry):
            pl.when(c == nm // 3)(sum_responses)
            pl.when(c == nm // 2)(weigh)

            @pl.when(c + ahead_m < nm)
            def _():
                gather_in(c + ahead_m)

            @pl.when(jnp.logical_or(jnp.logical_not(centre), c >= turns - 1))
            def _():
                finish(c)

            product = dot(mix[...], tot[:, span(c, wm)], PLAIN)
            kx[:, :, span(c, wm)] = kx[:, :, span(c, wm)] - product[:rows].reshape(
                PLANE, height, wm
            )
            lbuf[:, :, span(c, wm)] = product[rows:].reshape(PLANE, here, wm)
            for k in (3, 1, 2, 0):
                d_copy(c, k).start()
                l_copy(c, k).start()
            return carry

        lax.fori_loop(0, nm, deflate, 0)

        for d in range(1, cols):
            there = lax.rem(col + d, cols)
            done(next_in.at[there], n_recv.at[there])
        nxt[...] = jnp.sum(next_in[...], axis=0)

        for k in range(PLANE):
            done(deflated.at[:, pl.ds(pl.multiple_of(peers[k] * width, width), width)], d_recv.at[k])
            done(loadings.at[:, pl.ds(pl.multiple_of(peers[k] * width, width), width)], l_recv.at[k])
        for k in range(1, PLANE):
            done(kx.at[0], k_send.at[k])
            done(bq.at[0], b_send.at[k])
            done(kx.at[0], d_send.at[k])
            done(lbuf.at[0], l_send.at[k])
            done(t_own.at[0], t_send.at[k])
            done(t_full.at[0], tf_send.at[k])
            done(gram_full.at[0], gf_send.at[k])
        for d in range(1, group):
            other, _ = member(d)
            done(part.at[0], p_send.at[other])
            done(full.at[0], f_send.at[other])
        for d in range(1, planes):
            done(gram.at[0], g_send.at[plane_of(d)])
            done(t_sum, tz_send.at[plane_of(d)])
        for d in range(1, cols):
            done(next_own, n_send.at[lax.rem(col + d, cols)])

        def b_end(c, carry):
            for o in range(planes):

                @pl.when(jnp.logical_and(z < planes - 1, o <= z))
                def _(o=o):
                    done(bz_block(c, o), zb_send.at[1, c, o])

                @pl.when(jnp.logical_and(z > 0, o >= z))
                def _(o=o):
                    done(bz_block(c, o), zb_send.at[0, c, o])

            return carry

        lax.fori_loop(0, nk, b_end, 0)

        def m_end(c, carry):
            done(acc.at[:, span(c, wm)], in_send.at[c])

            @pl.when(has_outer)
            def _():
                done(tot.at[:, span(c, wm)], tot_send.at[c])

            return carry

        lax.fori_loop(0, nm, m_end, 0)

    f32 = jnp.float32
    dma = pltpu.SemaphoreType.DMA
    vmem = pl.BlockSpec(memory_space=pltpu.VMEM)
    hbm = pl.BlockSpec(memory_space=pltpu.HBM)
    anywhere = pl.BlockSpec(memory_space=pl.ANY)
    return pl.pallas_call(
        body,
        out_shape=[
            pltpu.VMEM((height, comp), f32),
            pltpu.VMEM((here, total), f32),
            pltpu.VMEM((resp, comp), f32),
            pltpu.VMEM((height, total), f32),
            pltpu.VMEM((height, comp), f32),
        ],
        in_specs=[hbm, hbm, vmem],
        out_specs=[vmem, anywhere, vmem, anywhere, vmem],
        scratch_shapes=[
            pltpu.VMEM((PLANE, height, width), f32),
            pltpu.VMEM((n, here, width), f32),
            pltpu.VMEM((comp, width), f32),
            pltpu.VMEM((comp, width), f32),
            pltpu.VMEM((comp, width), f32),
            pltpu.VMEM((PLANE, here, width), f32),
            pltpu.VMEM((group, slab, comp), f32),
            pltpu.VMEM((group, slab, comp), f32),
            pltpu.VMEM((group, slab, comp), f32),
            pltpu.VMEM((comp, rows), f32),
            pltpu.VMEM((PLANE, gram_slab, comp), f32),
            pltpu.VMEM((planes, gram_slab, comp), f32),
            pltpu.VMEM((gram_slab, comp), f32),
            pltpu.VMEM((PLANE, gram_slab, comp), f32),
            pltpu.VMEM((comp, 2 * comp), f32),
            pltpu.VMEM((comp, comp), f32),
            pltpu.VMEM((rows + here * PLANE, comp), f32),
            pltpu.VMEM((PLANE, resp_slab, comp), f32),
            pltpu.VMEM((PLANE, resp_slab, comp), f32),
            pltpu.VMEM((resp_slab, comp), f32),
            pltpu.VMEM((planes, resp_slab, comp), f32),
            pltpu.VMEM((PLANE, resp_slab, comp), f32),
            pltpu.VMEM((height, comp), f32),
            pltpu.VMEM((cols, height, comp), f32),
            dma((PLANE,)),
            dma((nk, PLANE)),
            dma((PLANE,)),
            dma((nk, PLANE)),
            dma((2, nk, planes)),
            dma((nk, planes)),
            dma((group,)),
            dma((group,)),
            dma((group,)),
            dma((group,)),
            dma((planes,)),
            dma((planes,)),
            dma((PLANE,)),
            dma((PLANE,)),
            dma((PLANE,)),
            dma((PLANE,)),
            dma((planes,)),
            dma((planes,)),
            dma((PLANE,)),
            dma((PLANE,)),
            dma((cols,)),
            dma((cols,)),
            dma((nm,)),
            dma((nm,)),
            dma((nm,)),
            dma((nm,)),
            dma((PLANE,)),
            dma((PLANE,)),
            dma((PLANE,)),
            dma((PLANE,)),
        ],
        compiler_params=pltpu.CompilerParams(
            collective_id=0, has_side_effects=True, vmem_limit_bytes=54 * 2**20
        ),
    )(kernel, basis_t, responses)


def hand_over(arrays):
    pieces = [(i, r) for i, a in enumerate(arrays) for r in range(0, a.shape[0], 8 if a.size > 2**18 else a.shape[0])]

    def body(*refs):
        count = len(arrays)
        sems = refs[-1]
        copies = []
        for j, (i, r) in enumerate(pieces):
            rows = pl.ds(r, 8 if arrays[i].size > 2**18 else arrays[i].shape[0])
            copies.append(
                pltpu.make_async_copy(refs[i].at[rows], refs[count + i].at[rows], sems.at[j])
            )
        for copy in copies:
            copy.start()
        for copy in copies:
            copy.wait()

    anywhere = pl.BlockSpec(memory_space=pl.ANY)
    return pl.pallas_call(
        body,
        out_shape=[jax.ShapeDtypeStruct(a.shape, a.dtype) for a in arrays],
        in_specs=[pl.BlockSpec(memory_space=pltpu.VMEM)] * len(arrays),
        out_specs=[anywhere] * len(arrays),
        scratch_shapes=[pltpu.SemaphoreType.DMA((len(pieces),))],
        compiler_params=pltpu.CompilerParams(vmem_limit_bytes=2**20),
    )(*arrays)


def local(kernel, basis, responses):
    return tuple(hand_over(step(kernel, basis.T, responses)))


def solution(mesh):
    return jax.shard_map(
        local,
        mesh=mesh,
        in_specs=(P("row", "col"), P("col", "row"), P("row", "col")),
        out_specs=(
            P("row", None),
            P("row", "col"),
            P("col", None),
            P("row", "col"),
            P("row", None),
        ),
        check_vma=False,
    )
```

```python
import math

import jax
import jax.numpy as jnp
from jax import lax
from jax.experimental import pallas as pl
from jax.experimental.pallas import tpu as pltpu
from jax.sharding import PartitionSpec as P

MESH = pl.DeviceIdType.MESH
HIGHEST = lax.Precision.HIGHEST
PLANE = 4
LAST = (((1,), (1,)), ((), ()))
FIRST = (((0,), (0,)), ((), ()))
PLAIN = (((1,), (0,)), ((), ()))


def dot(a, b, dims):
    return lax.dot_general(a, b, dims, precision=HIGHEST, preferred_element_type=jnp.float32)


def chunks_of(width, most):
    return max(c for c in range(1, most + 1) if width % (c * 128) == 0)


def remote(src, dst, send, recv, device):
    return pltpu.make_async_remote_copy(
        src_ref=src,
        dst_ref=dst,
        send_sem=send,
        recv_sem=recv,
        device_id=device,
        device_id_type=MESH,
    )


def done(ref, sem):
    pltpu.make_async_copy(ref, ref, sem).wait()


def inverse_factor(work, inverse, comp, tall, between):
    lane = lax.broadcasted_iota(jnp.int32, (tall, comp), 1)
    sub = lax.broadcasted_iota(jnp.int32, (tall, 1), 0)

    def panel(p, carry):
        top = pl.multiple_of(p * tall, tall)
        left = work[pl.ds(top, tall), :comp]
        right = work[pl.ds(top, tall), comp:]
        cols = [
            jnp.sum(jnp.where(lane == top + j, left, 0.0), axis=1, keepdims=True) for j in range(tall)
        ]
        for j in range(tall):
            pivot = cols[j][j : j + 1, :]
            scale = lax.rsqrt(pivot)
            scale = scale * (1.5 - 0.5 * pivot * scale * scale)
            mult = jnp.where(sub > j, cols[j] * scale, 0.0)
            left_row = left[j : j + 1, :] * scale
            right_row = right[j : j + 1, :] * scale
            left = jnp.where(sub == j, left_row, left - mult * left_row)
            right = jnp.where(sub == j, right_row, right - mult * right_row)
            for m in range(j + 1, tall):
                cols[m] = cols[m] - mult * (cols[m][j : j + 1, :] * scale)
        inverse[pl.ds(top, tall), :] = right
        work[...] = work[...] - dot(left, jnp.concatenate([left, right], axis=1), FIRST)
        between(p)
        return carry

    lax.fori_loop(0, comp // tall, panel, 0)


def step(kernel, basis_t, responses):
    n, cols = lax.axis_size("row"), lax.axis_size("col")
    planes = n // PLANE
    height, total = kernel.shape
    here = basis_t.shape[0]
    comp = here * n
    resp = responses.shape[1]
    width = total // PLANE
    rows = height * PLANE
    group = PLANE * cols
    slab = rows // group
    gram_slab = comp // PLANE
    resp_slab = resp // PLANE
    root_rows = math.sqrt(height * n)
    root_resp = math.sqrt(resp * cols)
    nk = chunks_of(width, 8)
    wk = width // nk
    nm = chunks_of(width, 32)
    wm = width // nm
    ahead_k, ahead_b = min(2, nk), min(2, nk)
    tall = 16
    every = 4
    turns = comp // tall // every
    half = planes // 2

    def body(
        k_hbm,
        b_hbm,
        resp_ref,
        scores,
        loadings,
        weights,
        deflated,
        nxt,
        kx,
        bq,
        acc,
        outer,
        tot,
        lbuf,
        part,
        part_in,
        full,
        full_t,
        gram,
        gram_in,
        gram_sum,
        gram_full,
        work,
        inverse,
        mix,
        t_own,
        t_in,
        t_sum,
        t_z,
        t_full,
        next_own,
        next_in,
        k_send,
        k_recv,
        b_send,
        b_recv,
        zb_send,
        zb_recv,
        p_send,
        p_recv,
        f_send,
        f_recv,
        g_send,
        g_recv,
        gf_send,
        gf_recv,
        t_send,
        t_recv,
        tz_send,
        tz_recv,
        tf_send,
        tf_recv,
        n_send,
        n_recv,
        in_send,
        in_recv,
        tot_send,
        tot_recv,
        d_send,
        d_recv,
        l_send,
        l_recv,
    ):
        me, col = lax.axis_index("row"), lax.axis_index("col")
        z, q = me // PLANE, me % PLANE
        y, x = q // 2, q % 2

        def peer(k):
            return (1 - y if k & 2 else y) * 2 + (1 - x if k & 1 else x)

        peers = [peer(k) for k in range(PLANE)]
        mine = q * cols + col

        def member(d):
            other = lax.rem(mine + d, group)
            return other, {"row": z * PLANE + other // cols, "col": other % cols}

        def plane_of(d):
            return lax.rem(z + d, planes)

        def above(f):
            pl.when(z < planes - 1)(f)

        def below(f):
            pl.when(z > 0)(f)

        def span(c, w):
            return pl.ds(pl.multiple_of(c * w, w), w)

        def quarter(k, c, w):
            return pl.ds(pl.multiple_of(peers[k] * width + c * w, w), w)

        def k_copy(c, k):
            src = k_hbm.at[:, quarter(k, c, wk)]
            dst = kx.at[q, :, span(c, wk)]
            if k == 0:
                return pltpu.make_async_copy(src, dst, k_recv.at[c, 0])
            return remote(
                src, dst, k_send.at[k], k_recv.at[c, k], {"row": z * PLANE + peers[k]}
            )

        def b_copy(c, k):
            src = b_hbm.at[:, quarter(k, c, wk)]
            dst = bq.at[me, :, span(c, wk)]
            if k == 0:
                return pltpu.make_async_copy(src, dst, b_recv.at[c, 0])
            return remote(
                src, dst, b_send.at[k], b_recv.at[c, k], {"row": z * PLANE + peers[k]}
            )

        def bz_block(c, origin):
            return bq.at[pl.ds(origin * PLANE, PLANE), :, span(c, wk)]

        def bz_copy(c, origin, way):
            ref = bz_block(c, origin)
            return remote(
                ref,
                ref,
                zb_send.at[(way + 1) // 2, c, origin],
                zb_recv.at[c, origin],
                {"row": me + way * PLANE},
            )

        def bz_first(c):
            for k in range(PLANE):
                done(bq.at[z * PLANE + peers[k], :, span(c, wk)], b_recv.at[c, k])

            @above
            def _():
                bz_copy(c, z, 1).start()

            @below
            def _():
                bz_copy(c, z, -1).start()

        def bz_relay(c):
            for d in range(1, planes):

                @pl.when(z - d >= 0)
                def _(d=d):
                    done(bz_block(c, z - d), zb_recv.at[c, z - d])

                    @above
                    def _():
                        bz_copy(c, z - d, 1).start()

                @pl.when(z + d < planes)
                def _(d=d):
                    done(bz_block(c, z + d), zb_recv.at[c, z + d])

                    @below
                    def _():
                        bz_copy(c, z + d, -1).start()

        b_own = [b_copy(c, 0) for c in range(nk)]
        for copy in b_own:
            copy.start()

        def k_own(c, carry):
            k_copy(c, 0).start()
            return carry

        lax.fori_loop(0, nk, k_own, 0)

        barrier = pltpu.get_barrier_semaphore()
        for d in range(1, group):
            pl.semaphore_signal(barrier, inc=1, device_id=member(d)[1], device_id_type=MESH)
        for d in range(1, planes):
            pl.semaphore_signal(
                barrier,
                inc=1,
                device_id={"row": plane_of(d) * PLANE + q},
                device_id_type=MESH,
            )
        pl.semaphore_wait(barrier, group + planes - 2)

        def b_start(c, carry):
            for k in range(1, PLANE):
                b_copy(c, k).start()
            return carry

        lax.fori_loop(0, nk, b_start, 0)
        for c in range(ahead_k):
            for k in range(1, PLANE):
                k_copy(c, k).start()
        for c in range(ahead_b):
            bz_first(c)
        part[...] = jnp.zeros_like(part)

        def project(c, carry):
            @pl.when(c + ahead_k < nk)
            def _():
                for k in range(1, PLANE):
                    k_copy(c + ahead_k, k).start()

            @pl.when(c + ahead_b < nk)
            def _():
                bz_first(c + ahead_b)

            bz_relay(c)
            for k in range(PLANE):
                done(kx.at[peers[k], :, span(c, wk)], k_recv.at[c, k])
            here_k = kx[:, :, span(c, wk)].reshape(rows, wk)
            here_b = bq[:, :, span(c, wk)].reshape(comp, wk)
            part[...] += dot(here_k, here_b, LAST).reshape(part.shape)
            return carry

        lax.fori_loop(0, nk, project, 0)

        for d in range(1, group):
            other, device = member(d)
            remote(
                part.at[other], part_in.at[mine], p_send.at[other], p_recv.at[mine], device
            ).start()
        total_rows = part[mine]
        for d in range(1, group):
            other, _ = member(d)
            done(part_in.at[other], p_recv.at[other])
            total_rows = total_rows + part_in[other]
        full[mine] = total_rows
        for d in range(1, group):
            other, device = member(d)
            remote(
                full.at[mine], full.at[mine], f_send.at[other], f_recv.at[mine], device
            ).start()
        for d in range(1, group):
            other, _ = member(d)
            done(full.at[other], f_recv.at[other])
        projected = full[...].reshape(rows, comp)

        gram[...] = dot(projected, projected, FIRST).reshape(gram.shape)

        def g_copy(d):
            return remote(
                gram.at[q],
                gram_in.at[z],
                g_send.at[plane_of(d)],
                g_recv.at[z],
                {"row": plane_of(d) * PLANE + q},
            )

        for d in range(1, planes):
            g_copy(d).start()
        gram_in[z] = gram[q]
        full_t[...] = projected.T

        lower = z < half
        inner_z = jnp.where(lower, z + 1, z - 1)
        outer_z = jnp.where(lower, z - 1, z + 1)
        centre = jnp.logical_or(z == half - 1, z == half)
        inward = {"row": inner_z * PLANE + q}
        outward = {"row": outer_z * PLANE + q}
        has_outer = jnp.logical_and(z > 0, z < planes - 1)

        def in_copy(c, to, recv):
            return remote(
                acc.at[:, span(c, wm)], to.at[:, span(c, wm)], in_send.at[c], recv.at[c], inward
            )

        def tot_copy(c):
            ref = tot.at[:, span(c, wm)]
            return remote(ref, ref, tot_send.at[c], tot_recv.at[c], outward)

        def gather_in(c):
            own = dot(full_t[...], kx[:, :, span(c, wm)].reshape(rows, wm), PLAIN)
            acc[:, span(c, wm)] = own

            @pl.when(has_outer)
            def _():
                done(outer.at[:, span(c, wm)], in_recv.at[c])
                acc[:, span(c, wm)] = acc[:, span(c, wm)] + outer[:, span(c, wm)]

            @pl.when(centre)
            def _():
                in_copy(c, tot, tot_recv).start()

            @pl.when(jnp.logical_not(centre))
            def _():
                in_copy(c, outer, in_recv).start()

        hops = jnp.where(lower, half - 1 - z, z - half)
        early = jnp.minimum(hops * 4, nm)
        ahead_m = jnp.minimum(turns + 1 + hops * 6, nm)

        def finish(c):
            done(tot.at[:, span(c, wm)], tot_recv.at[c])

            @pl.when(centre)
            def _():
                tot[:, span(c, wm)] = tot[:, span(c, wm)] + acc[:, span(c, wm)]

            @pl.when(has_outer)
            def _():
                tot_copy(c).start()

        def gather_some(first, last):
            def one(c, carry):
                gather_in(c)
                return carry

            lax.fori_loop(first, last, one, 0)

        gather_some(0, early)

        for d in range(1, planes):
            done(gram_in.at[plane_of(d)], g_recv.at[plane_of(d)])
        gram_full[q] = jnp.sum(gram_in[...], axis=0)

        def gf_copy(k):
            return remote(
                gram_full.at[q],
                gram_full.at[q],
                gf_send.at[k],
                gf_recv.at[k],
                {"row": z * PLANE + peers[k]},
            )

        for k in range(1, PLANE):
            gf_copy(k).start()

        own_rows = full[pl.ds(q * cols, cols)].reshape(height, comp)
        t_own[...] = dot(resp_ref[...], own_rows, FIRST).reshape(t_own.shape)
        for k in range(1, PLANE):
            remote(
                t_own.at[peers[k]],
                t_in.at[q],
                t_send.at[k],
                t_recv.at[k],
                {"row": z * PLANE + peers[k]},
            ).start()
        t_in[q] = t_own[q]
        first = jnp.maximum(early, 1)
        gather_some(early, first)
        for k in range(1, PLANE):
            done(gram_full.at[peers[k]], gf_recv.at[k])
        work[:, :comp] = gram_full[...].reshape(comp, comp) * (1.0 / (height * n))
        work[:, comp:] = (
            lax.broadcasted_iota(jnp.int32, (comp, comp), 0)
            == lax.broadcasted_iota(jnp.int32, (comp, comp), 1)
        ).astype(jnp.float32)

        def between(p):
            turn = p // every

            @pl.when(jnp.logical_and(p % every == every - 1, first + turn < nm))
            def _():
                gather_in(first + turn)

            @pl.when(jnp.logical_and(centre, jnp.logical_and(p % every == every - 1, turn > 0)))
            def _():
                finish(turn - 1)

        inverse_factor(work, inverse, comp, tall, between)
        plane_scores = dot(projected, inverse[...], LAST)
        mix[pl.ds(0, rows), :] = dot(plane_scores, inverse[...], PLAIN) * (1.0 / (height * n))
        mix[pl.ds(rows, here * PLANE), :] = inverse[
            pl.ds(pl.multiple_of(z * (here * PLANE), here * PLANE), here * PLANE), :
        ] * (1.0 / root_rows)

        for k in range(1, PLANE):
            done(t_in.at[peers[k]], t_recv.at[k])
        t_z[z] = jnp.sum(t_in[...], axis=0)
        t_sum[...] = t_z[z]
        for d in range(1, planes):
            remote(
                t_sum,
                t_z.at[z],
                tz_send.at[plane_of(d)],
                tz_recv.at[z],
                {"row": plane_of(d) * PLANE + q},
            ).start()

        gather_some(jnp.minimum(first + turns, nm), ahead_m)

        def d_copy(c, k):
            src = kx.at[peers[k], :, span(c, wm)]
            dst = deflated.at[:, quarter(0, c, wm)]
            if k == 0:
                return pltpu.make_async_copy(src, dst, d_recv.at[0])
            return remote(src, dst, d_send.at[k], d_recv.at[k], {"row": z * PLANE + peers[k]})

        def l_copy(c, k):
            src = lbuf.at[peers[k], :, span(c, wm)]
            dst = loadings.at[:, quarter(0, c, wm)]
            if k == 0:
                return pltpu.make_async_copy(src, dst, l_recv.at[0])
            return remote(src, dst, l_send.at[k], l_recv.at[k], {"row": z * PLANE + peers[k]})

        def sum_responses():
            for d in range(1, planes):
                done(t_z.at[plane_of(d)], tz_recv.at[plane_of(d)])
            t_full[q] = jnp.sum(t_z[...], axis=0)
            for k in range(1, PLANE):
                remote(
                    t_full.at[q],
                    t_full.at[q],
                    tf_send.at[k],
                    tf_recv.at[k],
                    {"row": z * PLANE + peers[k]},
                ).start()

        def weigh():
            scores[...] = dot(
                full[pl.ds(q * cols, cols)].reshape(height, comp), inverse[...], LAST
            )
            for k in range(1, PLANE):
                done(t_full.at[peers[k]], tf_recv.at[k])
            weights_here = dot(t_full[...].reshape(resp, comp), inverse[...], LAST) * (1.0 / root_rows)
            weights[...] = weights_here
            next_own[...] = dot(resp_ref[...], weights_here, PLAIN) * (1.0 / root_resp)
            next_in[col] = next_own[...]
            for d in range(1, cols):
                there = lax.rem(col + d, cols)
                remote(
                    next_own, next_in.at[col], n_send.at[there], n_recv.at[col], {"col": there}
                ).start()

        def deflate(c, carry):
            pl.when(c == nm // 3)(sum_responses)
            pl.when(c == nm // 2)(weigh)

            @pl.when(jnp.logical_or(jnp.logical_not(centre), c >= turns - 1))
            def _():
                finish(c)

            product = dot(mix[...], tot[:, span(c, wm)], PLAIN)
            kx[:, :, span(c, wm)] = kx[:, :, span(c, wm)] - product[:rows].reshape(
                PLANE, height, wm
            )
            lbuf[:, :, span(c, wm)] = product[rows:].reshape(PLANE, here, wm)
            for k in (3, 1, 2, 0):
                d_copy(c, k).start()
                l_copy(c, k).start()

            @pl.when(c + ahead_m < nm)
            def _():
                gather_in(c + ahead_m)
            return carry

        lax.fori_loop(0, nm, deflate, 0)

        for d in range(1, cols):
            there = lax.rem(col + d, cols)
            done(next_in.at[there], n_recv.at[there])
        nxt[...] = jnp.sum(next_in[...], axis=0)

        for k in range(PLANE):
            done(deflated.at[:, pl.ds(pl.multiple_of(peers[k] * width, width), width)], d_recv.at[k])
            done(loadings.at[:, pl.ds(pl.multiple_of(peers[k] * width, width), width)], l_recv.at[k])
        for k in range(1, PLANE):
            done(kx.at[0], k_send.at[k])
            done(bq.at[0], b_send.at[k])
            done(kx.at[0], d_send.at[k])
            done(lbuf.at[0], l_send.at[k])
            done(t_own.at[0], t_send.at[k])
            done(t_full.at[0], tf_send.at[k])
            done(gram_full.at[0], gf_send.at[k])
        for d in range(1, group):
            other, _ = member(d)
            done(part.at[0], p_send.at[other])
            done(full.at[0], f_send.at[other])
        for d in range(1, planes):
            done(gram.at[0], g_send.at[plane_of(d)])
            done(t_sum, tz_send.at[plane_of(d)])
        for d in range(1, cols):
            done(next_own, n_send.at[lax.rem(col + d, cols)])

        def b_end(c, carry):
            for o in range(planes):

                @pl.when(jnp.logical_and(z < planes - 1, o <= z))
                def _(o=o):
                    done(bz_block(c, o), zb_send.at[1, c, o])

                @pl.when(jnp.logical_and(z > 0, o >= z))
                def _(o=o):
                    done(bz_block(c, o), zb_send.at[0, c, o])

            return carry

        lax.fori_loop(0, nk, b_end, 0)

        def m_end(c, carry):
            done(acc.at[:, span(c, wm)], in_send.at[c])

            @pl.when(has_outer)
            def _():
                done(tot.at[:, span(c, wm)], tot_send.at[c])

            return carry

        lax.fori_loop(0, nm, m_end, 0)

    f32 = jnp.float32
    dma = pltpu.SemaphoreType.DMA
    vmem = pl.BlockSpec(memory_space=pltpu.VMEM)
    hbm = pl.BlockSpec(memory_space=pltpu.HBM)
    anywhere = pl.BlockSpec(memory_space=pl.ANY)
    return pl.pallas_call(
        body,
        out_shape=[
            pltpu.VMEM((height, comp), f32),
            pltpu.VMEM((here, total), f32),
            pltpu.VMEM((resp, comp), f32),
            pltpu.VMEM((height, total), f32),
            pltpu.VMEM((height, comp), f32),
        ],
        in_specs=[hbm, hbm, vmem],
        out_specs=[vmem, anywhere, vmem, anywhere, vmem],
        scratch_shapes=[
            pltpu.VMEM((PLANE, height, width), f32),
            pltpu.VMEM((n, here, width), f32),
            pltpu.VMEM((comp, width), f32),
            pltpu.VMEM((comp, width), f32),
            pltpu.VMEM((comp, width), f32),
            pltpu.VMEM((PLANE, here, width), f32),
            pltpu.VMEM((group, slab, comp), f32),
            pltpu.VMEM((group, slab, comp), f32),
            pltpu.VMEM((group, slab, comp), f32),
            pltpu.VMEM((comp, rows), f32),
            pltpu.VMEM((PLANE, gram_slab, comp), f32),
            pltpu.VMEM((planes, gram_slab, comp), f32),
            pltpu.VMEM((gram_slab, comp), f32),
            pltpu.VMEM((PLANE, gram_slab, comp), f32),
            pltpu.VMEM((comp, 2 * comp), f32),
            pltpu.VMEM((comp, comp), f32),
            pltpu.VMEM((rows + here * PLANE, comp), f32),
            pltpu.VMEM((PLANE, resp_slab, comp), f32),
            pltpu.VMEM((PLANE, resp_slab, comp), f32),
            pltpu.VMEM((resp_slab, comp), f32),
            pltpu.VMEM((planes, resp_slab, comp), f32),
            pltpu.VMEM((PLANE, resp_slab, comp), f32),
            pltpu.VMEM((height, comp), f32),
            pltpu.VMEM((cols, height, comp), f32),
            dma((PLANE,)),
            dma((nk, PLANE)),
            dma((PLANE,)),
            dma((nk, PLANE)),
            dma((2, nk, planes)),
            dma((nk, planes)),
            dma((group,)),
            dma((group,)),
            dma((group,)),
            dma((group,)),
            dma((planes,)),
            dma((planes,)),
            dma((PLANE,)),
            dma((PLANE,)),
            dma((PLANE,)),
            dma((PLANE,)),
            dma((planes,)),
            dma((planes,)),
            dma((PLANE,)),
            dma((PLANE,)),
            dma((cols,)),
            dma((cols,)),
            dma((nm,)),
            dma((nm,)),
            dma((nm,)),
            dma((nm,)),
            dma((PLANE,)),
            dma((PLANE,)),
            dma((PLANE,)),
            dma((PLANE,)),
        ],
        compiler_params=pltpu.CompilerParams(
            collective_id=0, has_side_effects=True, vmem_limit_bytes=54 * 2**20
        ),
    )(kernel, basis_t, responses)


def hand_over(arrays):
    pieces = [(i, r) for i, a in enumerate(arrays) for r in range(0, a.shape[0], 8 if a.size > 2**18 else a.shape[0])]

    def body(*refs):
        count = len(arrays)
        sems = refs[-1]
        copies = []
        for j, (i, r) in enumerate(pieces):
            rows = pl.ds(r, 8 if arrays[i].size > 2**18 else arrays[i].shape[0])
            copies.append(
                pltpu.make_async_copy(refs[i].at[rows], refs[count + i].at[rows], sems.at[j])
            )
        for copy in copies:
            copy.start()
        for copy in copies:
            copy.wait()

    anywhere = pl.BlockSpec(memory_space=pl.ANY)
    return pl.pallas_call(
        body,
        out_shape=[jax.ShapeDtypeStruct(a.shape, a.dtype) for a in arrays],
        in_specs=[pl.BlockSpec(memory_space=pltpu.VMEM)] * len(arrays),
        out_specs=[anywhere] * len(arrays),
        scratch_shapes=[pltpu.SemaphoreType.DMA((len(pieces),))],
        compiler_params=pltpu.CompilerParams(vmem_limit_bytes=2**20),
    )(*arrays)


def local(kernel, basis, responses):
    return tuple(hand_over(step(kernel, basis.T, responses)))


def solution(mesh):
    return jax.shard_map(
        local,
        mesh=mesh,
        in_specs=(P("row", "col"), P("col", "row"), P("row", "col")),
        out_specs=(
            P("row", None),
            P("row", "col"),
            P("col", None),
            P("row", "col"),
            P("row", None),
        ),
        check_vma=False,
    )
```

```python
import math

import jax
import jax.numpy as jnp
from jax import lax
from jax.experimental import pallas as pl
from jax.experimental.pallas import tpu as pltpu
from jax.sharding import PartitionSpec as P

MESH = pl.DeviceIdType.MESH
HIGHEST = lax.Precision.HIGHEST
PLANE = 4
LAST = (((1,), (1,)), ((), ()))
FIRST = (((0,), (0,)), ((), ()))
PLAIN = (((1,), (0,)), ((), ()))


def dot(a, b, dims):
    return lax.dot_general(a, b, dims, precision=HIGHEST, preferred_element_type=jnp.float32)


def chunks_of(width, most):
    return max(c for c in range(1, most + 1) if width % (c * 128) == 0)


def remote(src, dst, send, recv, device):
    return pltpu.make_async_remote_copy(
        src_ref=src,
        dst_ref=dst,
        send_sem=send,
        recv_sem=recv,
        device_id=device,
        device_id_type=MESH,
    )


def done(ref, sem):
    pltpu.make_async_copy(ref, ref, sem).wait()


def inverse_factor(work, inverse, comp, tall, between):
    lane = lax.broadcasted_iota(jnp.int32, (tall, comp), 1)
    sub = lax.broadcasted_iota(jnp.int32, (tall, 1), 0)

    def panel(p, carry):
        top = pl.multiple_of(p * tall, tall)
        left = work[pl.ds(top, tall), :comp]
        right = work[pl.ds(top, tall), comp:]
        cols = [
            jnp.sum(jnp.where(lane == top + j, left, 0.0), axis=1, keepdims=True) for j in range(tall)
        ]
        for j in range(tall):
            pivot = cols[j][j : j + 1, :]
            scale = lax.rsqrt(pivot)
            scale = scale * (1.5 - 0.5 * pivot * scale * scale)
            mult = jnp.where(sub > j, cols[j] * scale, 0.0)
            left_row = left[j : j + 1, :] * scale
            right_row = right[j : j + 1, :] * scale
            left = jnp.where(sub == j, left_row, left - mult * left_row)
            right = jnp.where(sub == j, right_row, right - mult * right_row)
            for m in range(j + 1, tall):
                cols[m] = cols[m] - mult * (cols[m][j : j + 1, :] * scale)
        inverse[pl.ds(top, tall), :] = right
        work[...] = work[...] - dot(left, jnp.concatenate([left, right], axis=1), FIRST)
        between(p)
        return carry

    lax.fori_loop(0, comp // tall, panel, 0)


def step(kernel, basis_t, responses):
    n, cols = lax.axis_size("row"), lax.axis_size("col")
    planes = n // PLANE
    height, total = kernel.shape
    here = basis_t.shape[0]
    comp = here * n
    resp = responses.shape[1]
    width = total // PLANE
    rows = height * PLANE
    group = PLANE * cols
    slab = rows // group
    gram_slab = comp // PLANE
    resp_slab = resp // PLANE
    root_rows = math.sqrt(height * n)
    root_resp = math.sqrt(resp * cols)
    nk = chunks_of(width, 8)
    wk = width // nk
    nm = chunks_of(width, 32)
    wm = width // nm
    ahead_k, ahead_b = min(2, nk), min(2, nk)
    tall = 16
    every = 4
    turns = comp // tall // every
    half = planes // 2

    def body(
        k_hbm,
        b_hbm,
        resp_hbm,
        scores,
        loadings,
        weights,
        deflated,
        nxt,
        resp_ref,
        resp_sem,
        kx,
        bq,
        acc,
        outer,
        tot,
        lbuf,
        part,
        part_in,
        full,
        full_t,
        gram,
        gram_in,
        gram_sum,
        gram_full,
        work,
        inverse,
        mix,
        t_own,
        t_in,
        t_sum,
        t_z,
        t_full,
        next_own,
        next_in,
        k_send,
        k_recv,
        b_send,
        b_recv,
        zb_send,
        zb_recv,
        p_send,
        p_recv,
        f_send,
        f_recv,
        g_send,
        g_recv,
        gf_send,
        gf_recv,
        t_send,
        t_recv,
        tz_send,
        tz_recv,
        tf_send,
        tf_recv,
        n_send,
        n_recv,
        in_send,
        in_recv,
        tot_send,
        tot_recv,
        d_send,
        d_recv,
        l_send,
        l_recv,
    ):
        me, col = lax.axis_index("row"), lax.axis_index("col")
        z, q = me // PLANE, me % PLANE
        y, x = q // 2, q % 2

        def peer(k):
            return (1 - y if k & 2 else y) * 2 + (1 - x if k & 1 else x)

        peers = [peer(k) for k in range(PLANE)]
        mine = q * cols + col

        def member(d):
            other = lax.rem(mine + d, group)
            return other, {"row": z * PLANE + other // cols, "col": other % cols}

        def plane_of(d):
            return lax.rem(z + d, planes)

        def above(f):
            pl.when(z < planes - 1)(f)

        def below(f):
            pl.when(z > 0)(f)

        def span(c, w):
            return pl.ds(pl.multiple_of(c * w, w), w)

        def quarter(k, c, w):
            return pl.ds(pl.multiple_of(peers[k] * width + c * w, w), w)

        def k_copy(c, k):
            src = k_hbm.at[:, quarter(k, c, wk)]
            dst = kx.at[q, :, span(c, wk)]
            if k == 0:
                return pltpu.make_async_copy(src, dst, k_recv.at[c, 0])
            return remote(
                src, dst, k_send.at[k], k_recv.at[c, k], {"row": z * PLANE + peers[k]}
            )

        def b_copy(c, k):
            src = b_hbm.at[:, quarter(k, c, wk)]
            dst = bq.at[me, :, span(c, wk)]
            if k == 0:
                return pltpu.make_async_copy(src, dst, b_recv.at[c, 0])
            return remote(
                src, dst, b_send.at[k], b_recv.at[c, k], {"row": z * PLANE + peers[k]}
            )

        def bz_block(c, origin):
            return bq.at[pl.ds(origin * PLANE, PLANE), :, span(c, wk)]

        def bz_copy(c, origin, way):
            ref = bz_block(c, origin)
            return remote(
                ref,
                ref,
                zb_send.at[(way + 1) // 2, c, origin],
                zb_recv.at[c, origin],
                {"row": me + way * PLANE},
            )

        def bz_first(c):
            for k in range(PLANE):
                done(bq.at[z * PLANE + peers[k], :, span(c, wk)], b_recv.at[c, k])

            @above
            def _():
                bz_copy(c, z, 1).start()

            @below
            def _():
                bz_copy(c, z, -1).start()

        def bz_relay(c):
            for d in range(1, planes):

                @pl.when(z - d >= 0)
                def _(d=d):
                    done(bz_block(c, z - d), zb_recv.at[c, z - d])

                    @above
                    def _():
                        bz_copy(c, z - d, 1).start()

                @pl.when(z + d < planes)
                def _(d=d):
                    done(bz_block(c, z + d), zb_recv.at[c, z + d])

                    @below
                    def _():
                        bz_copy(c, z + d, -1).start()

        resp_copy = pltpu.make_async_copy(resp_hbm, resp_ref, resp_sem)
        resp_copy.start()
        b_own = [b_copy(c, 0) for c in range(nk)]
        for copy in b_own:
            copy.start()

        def k_own(c, carry):
            k_copy(c, 0).start()
            return carry

        lax.fori_loop(0, nk, k_own, 0)

        barrier = pltpu.get_barrier_semaphore()
        for d in range(1, group):
            pl.semaphore_signal(barrier, inc=1, device_id=member(d)[1], device_id_type=MESH)
        for d in range(1, planes):
            pl.semaphore_signal(
                barrier,
                inc=1,
                device_id={"row": plane_of(d) * PLANE + q},
                device_id_type=MESH,
            )
        pl.semaphore_wait(barrier, group + planes - 2)

        def b_start(c, carry):
            for k in range(1, PLANE):
                b_copy(c, k).start()
            return carry

        lax.fori_loop(0, nk, b_start, 0)
        for c in range(ahead_k):
            for k in range(1, PLANE):
                k_copy(c, k).start()
        for c in range(ahead_b):
            bz_first(c)
        part[...] = jnp.zeros_like(part)

        def project(c, carry):
            @pl.when(c + ahead_k < nk)
            def _():
                for k in range(1, PLANE):
                    k_copy(c + ahead_k, k).start()

            @pl.when(c + ahead_b < nk)
            def _():
                bz_first(c + ahead_b)

            bz_relay(c)
            for k in range(PLANE):
                done(kx.at[peers[k], :, span(c, wk)], k_recv.at[c, k])
            here_k = kx[:, :, span(c, wk)].reshape(rows, wk)
            here_b = bq[:, :, span(c, wk)].reshape(comp, wk)
            part[...] += dot(here_k, here_b, LAST).reshape(part.shape)
            return carry

        lax.fori_loop(0, nk, project, 0)
        resp_copy.wait()

        for d in range(1, group):
            other, device = member(d)
            remote(
                part.at[other], part_in.at[mine], p_send.at[other], p_recv.at[mine], device
            ).start()
        total_rows = part[mine]
        for d in range(1, group):
            other, _ = member(d)
            done(part_in.at[other], p_recv.at[other])
            total_rows = total_rows + part_in[other]
        full[mine] = total_rows
        for d in range(1, group):
            other, device = member(d)
            remote(
                full.at[mine], full.at[mine], f_send.at[other], f_recv.at[mine], device
            ).start()
        for d in range(1, group):
            other, _ = member(d)
            done(full.at[other], f_recv.at[other])
        projected = full[...].reshape(rows, comp)

        gram[...] = dot(projected, projected, FIRST).reshape(gram.shape)

        def g_copy(d):
            return remote(
                gram.at[q],
                gram_in.at[z],
                g_send.at[plane_of(d)],
                g_recv.at[z],
                {"row": plane_of(d) * PLANE + q},
            )

        for d in range(1, planes):
            g_copy(d).start()
        gram_in[z] = gram[q]
        full_t[...] = projected.T

        lower = z < half
        inner_z = jnp.where(lower, z + 1, z - 1)
        outer_z = jnp.where(lower, z - 1, z + 1)
        centre = jnp.logical_or(z == half - 1, z == half)
        inward = {"row": inner_z * PLANE + q}
        outward = {"row": outer_z * PLANE + q}
        has_outer = jnp.logical_and(z > 0, z < planes - 1)

        def in_copy(c, to, recv):
            return remote(
                acc.at[:, span(c, wm)], to.at[:, span(c, wm)], in_send.at[c], recv.at[c], inward
            )

        def tot_copy(c):
            ref = tot.at[:, span(c, wm)]
            return remote(ref, ref, tot_send.at[c], tot_recv.at[c], outward)

        def gather_in(c):
            own = dot(full_t[...], kx[:, :, span(c, wm)].reshape(rows, wm), PLAIN)
            acc[:, span(c, wm)] = own

            @pl.when(has_outer)
            def _():
                done(outer.at[:, span(c, wm)], in_recv.at[c])
                acc[:, span(c, wm)] = acc[:, span(c, wm)] + outer[:, span(c, wm)]

            @pl.when(centre)
            def _():
                in_copy(c, tot, tot_recv).start()

            @pl.when(jnp.logical_not(centre))
            def _():
                in_copy(c, outer, in_recv).start()

        hops = jnp.where(lower, half - 1 - z, z - half)
        early = jnp.minimum(hops * 4, nm)
        ahead_m = jnp.minimum(turns + 1 + hops * 6, nm)

        def finish(c):
            done(tot.at[:, span(c, wm)], tot_recv.at[c])

            @pl.when(centre)
            def _():
                tot[:, span(c, wm)] = tot[:, span(c, wm)] + acc[:, span(c, wm)]

            @pl.when(has_outer)
            def _():
                tot_copy(c).start()

        def gather_some(first, last):
            def one(c, carry):
                gather_in(c)
                return carry

            lax.fori_loop(first, last, one, 0)

        gather_some(0, early)

        for d in range(1, planes):
            done(gram_in.at[plane_of(d)], g_recv.at[plane_of(d)])
        gram_full[q] = jnp.sum(gram_in[...], axis=0)

        def gf_copy(k):
            return remote(
                gram_full.at[q],
                gram_full.at[q],
                gf_send.at[k],
                gf_recv.at[k],
                {"row": z * PLANE + peers[k]},
            )

        for k in range(1, PLANE):
            gf_copy(k).start()

        own_rows = full[pl.ds(q * cols, cols)].reshape(height, comp)
        t_own[...] = dot(resp_ref[...], own_rows, FIRST).reshape(t_own.shape)
        for k in range(1, PLANE):
            remote(
                t_own.at[peers[k]],
                t_in.at[q],
                t_send.at[k],
                t_recv.at[k],
                {"row": z * PLANE + peers[k]},
            ).start()
        t_in[q] = t_own[q]
        first = jnp.maximum(early, 1)
        gather_some(early, first)
        for k in range(1, PLANE):
            done(gram_full.at[peers[k]], gf_recv.at[k])
        work[:, :comp] = gram_full[...].reshape(comp, comp) * (1.0 / (height * n))
        work[:, comp:] = (
            lax.broadcasted_iota(jnp.int32, (comp, comp), 0)
            == lax.broadcasted_iota(jnp.int32, (comp, comp), 1)
        ).astype(jnp.float32)

        def between(p):
            turn = p // every

            @pl.when(jnp.logical_and(p % every == every - 1, first + turn < nm))
            def _():
                gather_in(first + turn)

            @pl.when(jnp.logical_and(centre, jnp.logical_and(p % every == every - 1, turn > 0)))
            def _():
                finish(turn - 1)

        inverse_factor(work, inverse, comp, tall, between)
        plane_scores = dot(projected, inverse[...], LAST)
        mix[pl.ds(0, rows), :] = dot(plane_scores, inverse[...], PLAIN) * (1.0 / (height * n))
        mix[pl.ds(rows, here * PLANE), :] = inverse[
            pl.ds(pl.multiple_of(z * (here * PLANE), here * PLANE), here * PLANE), :
        ] * (1.0 / root_rows)

        for k in range(1, PLANE):
            done(t_in.at[peers[k]], t_recv.at[k])
        t_z[z] = jnp.sum(t_in[...], axis=0)
        t_sum[...] = t_z[z]
        for d in range(1, planes):
            remote(
                t_sum,
                t_z.at[z],
                tz_send.at[plane_of(d)],
                tz_recv.at[z],
                {"row": plane_of(d) * PLANE + q},
            ).start()

        gather_some(jnp.minimum(first + turns, nm), ahead_m)

        def d_copy(c, k):
            src = kx.at[peers[k], :, span(c, wm)]
            dst = deflated.at[:, quarter(0, c, wm)]
            if k == 0:
                return pltpu.make_async_copy(src, dst, d_recv.at[0])
            return remote(src, dst, d_send.at[k], d_recv.at[k], {"row": z * PLANE + peers[k]})

        def l_copy(c, k):
            src = lbuf.at[peers[k], :, span(c, wm)]
            dst = loadings.at[:, quarter(0, c, wm)]
            if k == 0:
                return pltpu.make_async_copy(src, dst, l_recv.at[0])
            return remote(src, dst, l_send.at[k], l_recv.at[k], {"row": z * PLANE + peers[k]})

        def sum_responses():
            for d in range(1, planes):
                done(t_z.at[plane_of(d)], tz_recv.at[plane_of(d)])
            t_full[q] = jnp.sum(t_z[...], axis=0)
            for k in range(1, PLANE):
                remote(
                    t_full.at[q],
                    t_full.at[q],
                    tf_send.at[k],
                    tf_recv.at[k],
                    {"row": z * PLANE + peers[k]},
                ).start()

        def weigh():
            scores[...] = dot(
                full[pl.ds(q * cols, cols)].reshape(height, comp), inverse[...], LAST
            )
            for k in range(1, PLANE):
                done(t_full.at[peers[k]], tf_recv.at[k])
            weights_here = dot(t_full[...].reshape(resp, comp), inverse[...], LAST) * (1.0 / root_rows)
            weights[...] = weights_here
            next_own[...] = dot(resp_ref[...], weights_here, PLAIN) * (1.0 / root_resp)
            next_in[col] = next_own[...]
            for d in range(1, cols):
                there = lax.rem(col + d, cols)
                remote(
                    next_own, next_in.at[col], n_send.at[there], n_recv.at[col], {"col": there}
                ).start()

        def deflate(c, carry):
            pl.when(c == nm // 3)(sum_responses)
            pl.when(c == nm // 2)(weigh)

            @pl.when(jnp.logical_or(jnp.logical_not(centre), c >= turns - 1))
            def _():
                finish(c)

            product = dot(mix[...], tot[:, span(c, wm)], PLAIN)
            kx[:, :, span(c, wm)] = kx[:, :, span(c, wm)] - product[:rows].reshape(
                PLANE, height, wm
            )
            lbuf[:, :, span(c, wm)] = product[rows:].reshape(PLANE, here, wm)
            for k in (3, 1, 2, 0):
                d_copy(c, k).start()
                l_copy(c, k).start()

            @pl.when(c + ahead_m < nm)
            def _():
                gather_in(c + ahead_m)
            return carry

        lax.fori_loop(0, nm, deflate, 0)

        for d in range(1, cols):
            there = lax.rem(col + d, cols)
            done(next_in.at[there], n_recv.at[there])
        nxt[...] = jnp.sum(next_in[...], axis=0)

        for k in range(PLANE):
            done(deflated.at[:, pl.ds(pl.multiple_of(peers[k] * width, width), width)], d_recv.at[k])
            done(loadings.at[:, pl.ds(pl.multiple_of(peers[k] * width, width), width)], l_recv.at[k])
        for k in range(1, PLANE):
            done(kx.at[0], k_send.at[k])
            done(bq.at[0], b_send.at[k])
            done(kx.at[0], d_send.at[k])
            done(lbuf.at[0], l_send.at[k])
            done(t_own.at[0], t_send.at[k])
            done(t_full.at[0], tf_send.at[k])
            done(gram_full.at[0], gf_send.at[k])
        for d in range(1, group):
            other, _ = member(d)
            done(part.at[0], p_send.at[other])
            done(full.at[0], f_send.at[other])
        for d in range(1, planes):
            done(gram.at[0], g_send.at[plane_of(d)])
            done(t_sum, tz_send.at[plane_of(d)])
        for d in range(1, cols):
            done(next_own, n_send.at[lax.rem(col + d, cols)])

        def b_end(c, carry):
            for o in range(planes):

                @pl.when(jnp.logical_and(z < planes - 1, o <= z))
                def _(o=o):
                    done(bz_block(c, o), zb_send.at[1, c, o])

                @pl.when(jnp.logical_and(z > 0, o >= z))
                def _(o=o):
                    done(bz_block(c, o), zb_send.at[0, c, o])

            return carry

        lax.fori_loop(0, nk, b_end, 0)

        def m_end(c, carry):
            done(acc.at[:, span(c, wm)], in_send.at[c])

            @pl.when(has_outer)
            def _():
                done(tot.at[:, span(c, wm)], tot_send.at[c])

            return carry

        lax.fori_loop(0, nm, m_end, 0)

    f32 = jnp.float32
    dma = pltpu.SemaphoreType.DMA
    vmem = pl.BlockSpec(memory_space=pltpu.VMEM)
    hbm = pl.BlockSpec(memory_space=pltpu.HBM)
    anywhere = pl.BlockSpec(memory_space=pl.ANY)
    return pl.pallas_call(
        body,
        out_shape=[
            pltpu.VMEM((height, comp), f32),
            pltpu.VMEM((here, total), f32),
            pltpu.VMEM((resp, comp), f32),
            pltpu.VMEM((height, total), f32),
            pltpu.VMEM((height, comp), f32),
        ],
        in_specs=[hbm, hbm, hbm],
        out_specs=[vmem, anywhere, vmem, anywhere, vmem],
        scratch_shapes=[
            pltpu.VMEM(responses.shape, f32),
            dma,
            pltpu.VMEM((PLANE, height, width), f32),
            pltpu.VMEM((n, here, width), f32),
            pltpu.VMEM((comp, width), f32),
            pltpu.VMEM((comp, width), f32),
            pltpu.VMEM((comp, width), f32),
            pltpu.VMEM((PLANE, here, width), f32),
            pltpu.VMEM((group, slab, comp), f32),
            pltpu.VMEM((group, slab, comp), f32),
            pltpu.VMEM((group, slab, comp), f32),
            pltpu.VMEM((comp, rows), f32),
            pltpu.VMEM((PLANE, gram_slab, comp), f32),
            pltpu.VMEM((planes, gram_slab, comp), f32),
            pltpu.VMEM((gram_slab, comp), f32),
            pltpu.VMEM((PLANE, gram_slab, comp), f32),
            pltpu.VMEM((comp, 2 * comp), f32),
            pltpu.VMEM((comp, comp), f32),
            pltpu.VMEM((rows + here * PLANE, comp), f32),
            pltpu.VMEM((PLANE, resp_slab, comp), f32),
            pltpu.VMEM((PLANE, resp_slab, comp), f32),
            pltpu.VMEM((resp_slab, comp), f32),
            pltpu.VMEM((planes, resp_slab, comp), f32),
            pltpu.VMEM((PLANE, resp_slab, comp), f32),
            pltpu.VMEM((height, comp), f32),
            pltpu.VMEM((cols, height, comp), f32),
            dma((PLANE,)),
            dma((nk, PLANE)),
            dma((PLANE,)),
            dma((nk, PLANE)),
            dma((2, nk, planes)),
            dma((nk, planes)),
            dma((group,)),
            dma((group,)),
            dma((group,)),
            dma((group,)),
            dma((planes,)),
            dma((planes,)),
            dma((PLANE,)),
            dma((PLANE,)),
            dma((PLANE,)),
            dma((PLANE,)),
            dma((planes,)),
            dma((planes,)),
            dma((PLANE,)),
            dma((PLANE,)),
            dma((cols,)),
            dma((cols,)),
            dma((nm,)),
            dma((nm,)),
            dma((nm,)),
            dma((nm,)),
            dma((PLANE,)),
            dma((PLANE,)),
            dma((PLANE,)),
            dma((PLANE,)),
        ],
        compiler_params=pltpu.CompilerParams(
            collective_id=0, has_side_effects=True, vmem_limit_bytes=56000 * 2**10
        ),
    )(kernel, basis_t, responses)


def hand_over(arrays):
    pieces = [(i, r) for i, a in enumerate(arrays) for r in range(0, a.shape[0], 8 if a.size > 2**18 else a.shape[0])]

    def body(*refs):
        count = len(arrays)
        sems = refs[-1]
        copies = []
        for j, (i, r) in enumerate(pieces):
            rows = pl.ds(r, 8 if arrays[i].size > 2**18 else arrays[i].shape[0])
            copies.append(
                pltpu.make_async_copy(refs[i].at[rows], refs[count + i].at[rows], sems.at[j])
            )
        for copy in copies:
            copy.start()
        for copy in copies:
            copy.wait()

    anywhere = pl.BlockSpec(memory_space=pl.ANY)
    return pl.pallas_call(
        body,
        out_shape=[jax.ShapeDtypeStruct(a.shape, a.dtype) for a in arrays],
        in_specs=[pl.BlockSpec(memory_space=pltpu.VMEM)] * len(arrays),
        out_specs=[anywhere] * len(arrays),
        scratch_shapes=[pltpu.SemaphoreType.DMA((len(pieces),))],
        compiler_params=pltpu.CompilerParams(vmem_limit_bytes=2**20),
    )(*arrays)


def local(kernel, basis, responses):
    return tuple(hand_over(step(kernel, basis.T, responses)))


def solution(mesh):
    return jax.shard_map(
        local,
        mesh=mesh,
        in_specs=(P("row", "col"), P("col", "row"), P("row", "col")),
        out_specs=(
            P("row", None),
            P("row", "col"),
            P("col", None),
            P("row", "col"),
            P("row", None),
        ),
        check_vma=False,
    )
```
